32 devices in a mesh: rep: 2 (over y), space: 4 (over z), tm: 4 (over x, core).
Axes of the slice: x: 2, y: 2, z: 4, core: 2. Of those that a mesh axis runs over, the one named last changes fastest.
Arguments:
- inputs: bfloat16 [16, 4, 96, 192], P(('rep', 'tm'), 'space'), parts along dimension 0, may hold values from -6 to 6
- cotangent: bfloat16 [16, 4, 96, 192], P(('rep', 'tm'), 'space'), parts along dimension 0, may hold values from -6 to 6
- weight: bfloat16 [3, 3, 3, 192, 192], replicated, may hold values from -0.078125 to 0.078125
Outputs:
- input_grad: bfloat16 [16, 4, 96, 192], P(('rep', 'tm'), 'space'), parts along dimension 0
- weight_grad: float32 [3, 3, 3, 384, 192], P(None, None, None, ('rep', 'tm'), 'space'), parts along dimension 3
The draws below stay inside these ranges and needn't reach their ends.
There are 2 independent parts, one for each index of `rep`. The reference program is written for one: setup_inputs(seed, part) draws one part's arguments, and reference() takes and returns one part's arrays. A program takes and returns all parts, laid end to end along the dimension named above; an argument that names none is the same for every part. Nothing has to cross between parts.
All inputs are finite; a program needn't handle non-finite values.
Results may differ from the reference program's by a relative error of at most 0.0049.
Values may be sent and summed in bfloat16 or wider, within the bound.
A program may use at most 128 MiB of HBM per device.

```python
import math
import jax
import jax.numpy as jnp
from jax import lax

CIN = 192
COUT = 192
WIDTH = 96
FRAMES = 8
HEIGHT = 4


def strengthened(values, key, source, target, shards_of, factor):
    def block_of(axis_at):
        return (jnp.arange(values.shape[axis_at]) // (values.shape[axis_at] // shards_of)).reshape((-1,) + (1,) * (values.ndim - 1 - axis_at))

    first = jax.random.permutation(key, shards_of)[block_of(target)]
    second = (block_of(target) + shards_of // 2) % shards_of
    return jnp.where((block_of(source) == first) | (block_of(source) == second), factor * values, values)


def level_of(own_key, extent, cuts, least, largest):
    gain, own = 1.0, jax.random.fold_in(own_key, 6)
    for position, blocks in cuts:
        steps = jnp.exp(jax.random.uniform(jax.random.fold_in(own, position), (blocks,), jnp.float32, least / len(cuts), largest / len(cuts)))
        gain = gain * jnp.repeat(steps, extent[position] // blocks).reshape([-1 if axis == position else 1 for axis in range(len(extent))])
    return gain


def normal_values(rng, dims, spread, reach, pieces=(), held_as=jnp.bfloat16):
    gain = level_of(rng, dims, pieces, -0.22, 0.18) if pieces else 1.0
    entries = jax.random.normal(rng, dims, jnp.float32) * spread * gain
    return jnp.minimum(jnp.maximum(entries, -reach), reach).astype(held_as)


def gaussian_with(stream_key, dims, spread, reach, cuts, heavy, kind=jnp.bfloat16):
    result = spread * jax.random.normal(stream_key, dims, jnp.float32)
    if cuts:
        result = result * level_of(stream_key, dims, cuts, -0.22, 0.18)
    return jnp.clip(strengthened(result, jax.random.fold_in(stream_key, 3), *heavy), -reach, reach).astype(kind)


def setup_inputs(seed: int = 0, part: int = 0) -> dict:
    key_of = jax.random.split(jax.random.key(seed), 4)
    part_keys = jax.random.split(jax.random.fold_in(key_of[3], part), 4)
    inputs = gaussian_with(part_keys[0], (FRAMES, HEIGHT, WIDTH, CIN), 1.0, 6.0, ((0, 4), (1, 4)), (0, 3, 4, 2.0))
    cotangent = gaussian_with(part_keys[1], (FRAMES, HEIGHT, WIDTH, COUT), 1.0, 6.0, ((0, 4), (1, 4)), (1, 3, 4, 2.0))
    weight = normal_values(key_of[2], (3, 3, 3, CIN, COUT), (27 * CIN) ** -0.5, 0.078125)
    return {"inputs": inputs, "cotangent": cotangent, "weight": weight}


def reference(inputs, cotangent, weight):
    cell_count = FRAMES * HEIGHT * WIDTH
    padded = jnp.pad(inputs, ((2, 0), (1, 1), (1, 1), (0, 0)))
    outputs = jnp.zeros((cell_count, COUT), jnp.float32)
    for depth_tap in range(3):
        for row_tap in range(3):
            for col_tap in range(3):
                window = padded[depth_tap:depth_tap + FRAMES, row_tap:row_tap + HEIGHT, col_tap:col_tap + WIDTH].reshape(cell_count, CIN)
                outputs = outputs + jnp.dot(window, weight[depth_tap, row_tap, col_tap], preferred_element_type=jnp.float32)
    logistic = jax.nn.sigmoid(outputs)
    derivative = logistic * (1.0 + outputs * (1.0 - logistic))
    upstream = (cotangent.reshape(cell_count, COUT).astype(jnp.float32) * derivative).astype(jnp.bfloat16)
    following = jnp.pad(upstream.reshape(FRAMES, HEIGHT, WIDTH, COUT), ((0, 2), (1, 1), (1, 1), (0, 0)))
    input_grad = jnp.zeros((cell_count, CIN), jnp.float32)
    tap_grads = []
    for depth_tap in range(3):
        for row_tap in range(3):
            for col_tap in range(3):
                returned = following[2 - depth_tap:2 - depth_tap + FRAMES, 2 - row_tap:2 - row_tap + HEIGHT, 2 - col_tap:2 - col_tap + WIDTH].reshape(cell_count, COUT)
                input_grad = input_grad + lax.dot_general(returned, weight[depth_tap, row_tap, col_tap], (((1,), (1,)), ((), ())), preferred_element_type=jnp.float32)
                window = padded[depth_tap:depth_tap + FRAMES, row_tap:row_tap + HEIGHT, col_tap:col_tap + WIDTH].reshape(cell_count, CIN)
                tap_grads.append(lax.dot_general(window, upstream, (((0,), (0,)), ((), ())), preferred_element_type=jnp.float32))
    weight_grad = jnp.stack(tap_grads).reshape(3, 3, 3, CIN, COUT) * (1.0 / math.sqrt(cell_count))
    return (input_grad.reshape(FRAMES, HEIGHT, WIDTH, CIN).astype(jnp.bfloat16), weight_grad)
```

```python
import functools
import math

import jax
import jax.numpy as jnp
from jax import lax
from jax.experimental import pallas as pl
from jax.experimental.pallas import tpu as pltpu
from jax.sharding import PartitionSpec as P

MESH = pl.DeviceIdType.MESH
LANES = 128


def passed_along(array, axis, by):
    length = lax.axis_size(axis)
    pairs = [(i, i + by) for i in range(length) if 0 <= i + by < length]
    return lax.ppermute(array, axis, pairs)


def extended_2(cells, sides, width):
    for axis, dim in sides:
        count = lax.axis_size(axis)
        ends = count - 1
        head = lax.slice_in_dim(cells, 0, width, axis=dim)
        tail = lax.slice_in_dim(cells, cells.shape[dim] - width, cells.shape[dim], axis=dim)
        cells = jnp.concatenate(
            [
                lax.ppermute(tail, axis, [(i, (i + 1) % count) for i in range(ends)]),
                cells,
                lax.ppermute(head, axis, [((i + 1) % count, i) for i in range(ends)]),
            ],
            axis=dim,
        )
    return cells


def reduced(inputs, cotangent, weight):
    frame_count, row_count, col_count, in_channels = inputs.shape
    out_channels = cotangent.shape[3]
    cell_count = frame_count * row_count * col_count
    space_size = lax.axis_size("space")
    time_size = lax.axis_size("tm")
    factor = 1.0 / math.sqrt(cell_count * space_size * time_size)
    earlier = passed_along(inputs, "tm", 1)
    extended = jnp.concatenate([earlier, inputs], axis=0)
    rimmed = extended_2(extended, (("space", 1),), 1)
    padded = jnp.pad(rimmed, ((0, 0), (0, 0), (1, 1), (0, 0)))
    outputs = jnp.zeros((cell_count, out_channels), jnp.float32)
    for depth_tap in range(3):
        for row_tap in range(3):
            for col_tap in range(3):
                window = padded[
                    depth_tap : depth_tap + frame_count,
                    row_tap : row_tap + row_count,
                    col_tap : col_tap + col_count,
                ].reshape(cell_count, in_channels)
                outputs = outputs + jnp.dot(
                    window, weight[depth_tap, row_tap, col_tap], preferred_element_type=jnp.float32
                )
    logistic = jax.nn.sigmoid(outputs)
    derivative = logistic * (1.0 + outputs * (1.0 - logistic))
    upstream = (
        cotangent.reshape(cell_count, out_channels).astype(jnp.float32) * derivative
    ).astype(jnp.bfloat16)
    upstream_grid = upstream.reshape(frame_count, row_count, col_count, out_channels)
    arriving = passed_along(upstream_grid, "tm", -1)
    following = jnp.concatenate([upstream_grid, arriving], axis=0)
    following = extended_2(following, (("space", 1),), 1)
    following = jnp.pad(following, ((0, 0), (0, 0), (1, 1), (0, 0)))
    input_grad = jnp.zeros((cell_count, in_channels), jnp.float32)
    tap_grads = []
    for depth_tap in range(3):
        for row_tap in range(3):
            for col_tap in range(3):
                returned = following[
                    2 - depth_tap : 2 - depth_tap + frame_count,
                    2 - row_tap : 2 - row_tap + row_count,
                    2 - col_tap : 2 - col_tap + col_count,
                ].reshape(cell_count, out_channels)
                input_grad = input_grad + lax.dot_general(
                    returned,
                    weight[depth_tap, row_tap, col_tap],
                    (((1,), (1,)), ((), ())),
                    preferred_element_type=jnp.float32,
                )
                window = padded[
                    depth_tap : depth_tap + frame_count,
                    row_tap : row_tap + row_count,
                    col_tap : col_tap + col_count,
                ].reshape(cell_count, in_channels)
                tap_grads.append(
                    lax.dot_general(
                        window,
                        upstream,
                        (((0,), (0,)), ((), ())),
                        preferred_element_type=jnp.float32,
                    )
                )
    partial_grad = jnp.stack(tap_grads) * factor
    in_share = in_channels // time_size
    out_share = out_channels // space_size
    blocks = partial_grad.reshape(27, in_channels, space_size, out_share)
    blocks = blocks.transpose(2, 0, 1, 3).reshape(space_size * 27, in_channels, out_share)
    spatial_sum = lax.psum_scatter(blocks, "space", scatter_dimension=0, tiled=True)
    blocks = spatial_sum.reshape(27, time_size, in_share, out_share)
    blocks = blocks.transpose(1, 0, 2, 3).reshape(time_size * 27, in_share, out_share)
    owned_part = lax.psum_scatter(blocks, "tm", scatter_dimension=0, tiled=True)
    input_grad = input_grad.reshape(frame_count, row_count, col_count, in_channels).astype(
        jnp.bfloat16
    )
    return (input_grad, owned_part.reshape(3, 3, 3, in_share, out_share))


def shifted_rows(values, by, width):
    count = values.shape[0]
    rows = lax.broadcasted_iota(jnp.int32, values.shape, 0)
    edge = 0 if by < 0 else width - 1
    outside = rows == edge
    for frame in range(1, count // width):
        outside = outside | (rows == frame * width + edge)
    moved = pltpu.roll(values, 1 if by < 0 else count - 1, 0)
    return jnp.where(outside, 0.0, moved)


def transposed_slices(values, width, share, store):
    frames = values.shape[0] // width
    channels = values.shape[1]
    for frame in range(frames):
        part = values[frame * width : (frame + 1) * width]
        part = jnp.concatenate([part, jnp.zeros((LANES - width, channels), part.dtype)], axis=0)
        turned = part.T.astype(jnp.bfloat16)
        for piece in range(channels // share):
            store(piece, frame * share, turned[piece * share : (piece + 1) * share])


def kernel(
    space, time, width, factor,
    x_ref, g_ref, w_hbm, ig_ref, wg_ref,
    w_ref, xbuf, ubuf, xts, uts, xrecv, urecv, xb,
    w_sem, hx_send, hx_recv, hu_send, hu_recv,
    x1_send, x1_recv, x2_send, x2_recv, u1_send, u1_recv, u2_send, u2_recv,
):
    z = lax.axis_index("space")
    t = lax.axis_index("tm")
    cells, cin = x_ref.shape
    cout = g_ref.shape[1]
    in_share, out_share = cin // time, cout // space
    frames = cells // width
    lanes = space * LANES
    weight_copy = pltpu.make_async_copy(w_hbm, w_ref, w_sem)
    weight_copy.start()

    below, above = z > 0, z < space - 1
    early, late = t > 0, t < time - 1
    diagonals = (
        (below & early, -1, -1), (below & late, -1, 1), (above & early, 1, -1), (above & late, 1, 1),
    )

    def at(dz, dt):
        return {"space": z + dz, "tm": t + dt}

    barrier = pltpu.get_barrier_semaphore()
    for step in range(1, space):
        pl.semaphore_signal(
            barrier, 1, device_id={"space": lax.rem(z + step, space), "tm": t}, device_id_type=MESH
        )
    for step in range(1, time):
        pl.semaphore_signal(
            barrier, 1, device_id={"space": z, "tm": lax.rem(t + step, time)}, device_id_type=MESH
        )
    for there, dz, dt in diagonals:
        @pl.when(there)
        def _(dz=dz, dt=dt):
            pl.semaphore_signal(barrier, 1, device_id=at(dz, dt), device_id_type=MESH)

    own = x_ref[...]
    xbuf[1, cells:] = own

    def keep_x(piece, row, block):
        xts[piece, pl.ds(row, in_share)] = block

    transposed_slices(own.astype(jnp.float32), width, in_share, keep_x)
    xrecv[z, t] = xts[t]
    urecv[:, time * lanes :] = jnp.zeros((frames * out_share, lanes), jnp.bfloat16)
    block = (cells, cin)

    @pl.when(jnp.logical_not(early))
    def _():
        for row in range(3):
            xbuf[row, :cells] = jnp.zeros(block, jnp.bfloat16)

    @pl.when(jnp.logical_not(late))
    def _():
        for row in range(3):
            ubuf[row, cells:] = jnp.zeros((cells, cout), jnp.bfloat16)

    for missing, row in ((jnp.logical_not(below), 0), (jnp.logical_not(above), 2)):
        @pl.when(missing)
        def _(row=row):
            xbuf[row] = jnp.zeros((2 * cells, cin), jnp.bfloat16)
            ubuf[row] = jnp.zeros((2 * cells, cout), jnp.bfloat16)

    beside = (z + space - 1) // space + (2 * space - 2 - z) // space
    around = (t + time - 1) // time + (2 * time - 2 - t) // time
    pl.semaphore_wait(barrier, space + time - 2 + beside * around)

    def halo(source, buf, send, recv, slot, row, half, there, dz, dt):
        copy = pltpu.make_async_remote_copy(
            src_ref=source,
            dst_ref=buf.at[row, pl.ds(half * cells, cells)],
            send_sem=send.at[slot],
            recv_sem=recv.at[slot],
            device_id=at(dz, dt),
            device_id_type=MESH,
        )
        return there, copy

    def start(pair):
        @pl.when(pair[0])
        def _():
            pair[1].start()

    def received(here, copy):
        @pl.when(here)
        def _():
            copy.wait_recv()

    x_halo = (
        (halo(x_ref, xbuf, hx_send, hx_recv, 0, 1, 0, late, 0, 1), early),
        (halo(x_ref, xbuf, hx_send, hx_recv, 1, 0, 1, above, 1, 0), below),
        (halo(x_ref, xbuf, hx_send, hx_recv, 2, 2, 1, below, -1, 0), above),
        (halo(x_ref, xbuf, hx_send, hx_recv, 3, 0, 0, above & late, 1, 1), below & early),
        (halo(x_ref, xbuf, hx_send, hx_recv, 4, 2, 0, below & late, -1, 1), above & early),
    )
    for pair, _ in x_halo:
        start(pair)

    def exchange(source, target, send, recv, slot, mine, device):
        return pltpu.make_async_remote_copy(
            src_ref=source, dst_ref=target, send_sem=send.at[slot], recv_sem=recv.at[slot],
            device_id=device, device_id_type=MESH,
        )

    x1, x2, u1, u2 = [], [], [], []
    for step in range(1, time):
        other = lax.rem(t + step, time)
        x1.append(exchange(xts.at[other], xrecv.at[z, t], x1_send, x1_recv, step - 1, t,
                           {"space": z, "tm": other}))
        window = urecv.at[:, pl.ds(pl.multiple_of(t * lanes, LANES), lanes)]
        u2.append(exchange(window, window, u2_send, u2_recv, step - 1, t, {"space": z, "tm": other}))
    for step in range(1, space):
        other = lax.rem(z + step, space)
        x2.append(exchange(xrecv.at[z], xrecv.at[z], x2_send, x2_recv, step - 1, z,
                           {"space": other, "tm": t}))
        window = urecv.at[:, pl.ds(pl.multiple_of(t * lanes + z * LANES, LANES), LANES)]
        u1.append(exchange(uts.at[other], window, u1_send, u1_recv, step - 1, z,
                           {"space": other, "tm": t}))
    for copy in x1:
        copy.start()

    def taps(buf, row, tap_row, forward, totals):
        for depth in range(3):
            offset = (depth if forward else 2 - depth) * width
            window = buf[row, offset : offset + cells]
            for col in range(3):
                tap = w_ref[(depth * 3 + tap_row) * 3 + col]
                product = lax.dot_general(
                    window, tap, (((1,), (0 if forward else 1,)), ((), ())),
                    preferred_element_type=jnp.float32,
                )
                totals[col] = product if totals[col] is None else totals[col] + product

    weight_copy.wait()
    sums = [None, None, None]
    received(x_halo[0][1], x_halo[0][0][1])
    taps(xbuf, 1, 1, True, sums)
    for copy in x1:
        copy.wait_recv()
    for copy in x2:
        copy.start()
    for (_, copy), here in x_halo[1:]:
        received(here, copy)
    taps(xbuf, 0, 0, True, sums)
    taps(xbuf, 2, 2, True, sums)
    outputs = shifted_rows(sums[0], -1, width) + sums[1] + shifted_rows(sums[2], 1, width)
    logistic = jax.nn.sigmoid(outputs)
    derivative = logistic * (1.0 + outputs * (1.0 - logistic))
    upstream = (g_ref[...].astype(jnp.float32) * derivative).astype(jnp.bfloat16)
    ubuf[1, :cells] = upstream

    def keep_u(piece, row, block):
        uts[piece, pl.ds(row, out_share)] = block

    transposed_slices(upstream.astype(jnp.float32), width, out_share, keep_u)
    urecv[:, pl.ds(pl.multiple_of(t * lanes + z * LANES, LANES), LANES)] = uts[z]
    for copy in u1:
        copy.start()
    u_own = ubuf.at[1, pl.ds(0, cells)]
    u_halo = (
        (halo(u_own, ubuf, hu_send, hu_recv, 0, 1, 1, early, 0, -1), late),
        (halo(u_own, ubuf, hu_send, hu_recv, 1, 0, 0, above, 1, 0), below),
        (halo(u_own, ubuf, hu_send, hu_recv, 2, 2, 0, below, -1, 0), above),
        (halo(u_own, ubuf, hu_send, hu_recv, 3, 0, 1, above & early, 1, -1), below & late),
        (halo(u_own, ubuf, hu_send, hu_recv, 4, 2, 1, below & early, -1, -1), above & late),
    )
    for pair, _ in u_halo:
        start(pair)

    for copy in x2:
        copy.wait_recv()
    for pair_at in range(time):
        base = pair_at * lanes
        nothing = jnp.zeros((frames * in_share, LANES), jnp.bfloat16)
        for col in range(3):
            xb[col, :, base : base + LANES] = nothing
            xb[6 + col, :, base + lanes - LANES : base + lanes] = nothing
        for row in range(space):
            held = xrecv[row, pair_at]
            wide = held.astype(jnp.float32)
            moved = (
                pltpu.roll(wide, 1, 1).astype(jnp.bfloat16),
                held,
                pltpu.roll(wide, LANES - 1, 1).astype(jnp.bfloat16),
            )
            for tap_row in range(3):
                place = row - tap_row + 1
                if 0 <= place < space:
                    for col in range(3):
                        xb[tap_row * 3 + col, :, base + place * LANES : base + (place + 1) * LANES] = moved[col]

    for copy in u1:
        copy.wait_recv()
    for copy in u2:
        copy.start()

    sums = [None, None, None]
    received(u_halo[0][1], u_halo[0][0][1])
    taps(ubuf, 1, 1, False, sums)
    for (_, copy), here in u_halo[1:]:
        received(here, copy)
    taps(ubuf, 0, 2, False, sums)
    taps(ubuf, 2, 0, False, sums)
    total = shifted_rows(sums[0], 1, width) + sums[1] + shifted_rows(sums[2], -1, width)
    ig_ref[...] = total.astype(jnp.bfloat16)

    for copy in u2:
        copy.wait_recv()
    both = jnp.concatenate([urecv[:, : time * lanes], urecv[:, lanes:]], axis=0)
    for tap_row in range(3):
        left = xb[tap_row * 3 : tap_row * 3 + 3].reshape(3 * frames * in_share, time * lanes)
        grads = lax.dot_general(
            left, both, (((1,), (1,)), ((), ())), preferred_element_type=jnp.float32
        ) * factor
        grads = grads.reshape(3, frames, in_share, 2 * frames * out_share)
        for col in range(3):
            joined = grads[col, 0, :, : 3 * out_share] + grads[col, 1, :, out_share:]
            for depth in range(3):
                lag = 2 - depth
                wg_ref[(depth * 3 + tap_row) * 3 + col] = joined[:, lag * out_share : (lag + 1) * out_share]

    for copy in x1 + x2 + u1 + u2:
        copy.wait_send()
    for pair, _ in x_halo + u_halo:
        @pl.when(pair[0])
        def _(copy=pair[1]):
            copy.wait_send()


def gathered(space, time, inputs, cotangent, weight):
    frames, _, width, cin = inputs.shape
    cout = cotangent.shape[3]
    cells = frames * width
    in_share, out_share = cin // time, cout // space
    lanes = space * LANES
    factor = 1.0 / math.sqrt(cells * space * time)
    vmem = pl.BlockSpec(memory_space=pltpu.VMEM)
    dma = pltpu.SemaphoreType.DMA
    bf16 = jnp.bfloat16
    input_grad, weight_grad = pl.pallas_call(
        functools.partial(kernel, space, time, width, factor),
        out_shape=(
            jax.ShapeDtypeStruct((cells, cin), bf16),
            jax.ShapeDtypeStruct((27, in_share, out_share), jnp.float32),
        ),
        in_specs=[vmem, vmem, pl.BlockSpec(memory_space=pl.ANY)],
        out_specs=(vmem, vmem),
        scratch_shapes=[
            pltpu.VMEM((27, cin, cout), bf16),
            pltpu.VMEM((3, 2 * cells, cin), bf16),
            pltpu.VMEM((3, 2 * cells, cout), bf16),
            pltpu.VMEM((time, frames * in_share, LANES), bf16),
            pltpu.VMEM((space, frames * out_share, LANES), bf16),
            pltpu.VMEM((space, time, frames * in_share, LANES), bf16),
            pltpu.VMEM((frames * out_share, (time + 1) * lanes), bf16),
            pltpu.VMEM((9, frames * in_share, time * lanes), bf16),
            dma,
            dma((5,)), dma((5,)), dma((5,)), dma((5,)),
            dma((time - 1,)), dma((time - 1,)), dma((space - 1,)), dma((space - 1,)),
            dma((space - 1,)), dma((space - 1,)), dma((time - 1,)), dma((time - 1,)),
        ],
        compiler_params=pltpu.CompilerParams(
            collective_id=0, has_side_effects=True, vmem_limit_bytes=62 * 1024 * 1024
        ),
    )(inputs.reshape(cells, cin), cotangent.reshape(cells, cout), weight.reshape(27, cin, cout))
    return (
        input_grad.reshape(inputs.shape),
        weight_grad.reshape(3, 3, 3, in_share, out_share),
    )


def local(space, time, inputs, cotangent, weight):
    frames, rows, width, cin = inputs.shape
    cout = cotangent.shape[3]
    slices = 2 * frames * rows * width * space * time * (cin // time + cout // space)
    partials = 4 * 27 * cin * cout
    fits = (
        frames == 2
        and rows == 1
        and width < LANES
        and width % 16 == 0
        and space > 1
        and time > 1
        and (cin // time) % 16 == 0
        and (cout // space) % 16 == 0
    )
    if fits and slices < partials:
        return gathered(space, time, inputs, cotangent, weight)
    return reduced(inputs, cotangent, weight)


def solution(mesh):
    placed = (P(("rep", "tm"), "space", None, None), P(("rep", "tm"), "space", None, None), P())
    return jax.shard_map(
        functools.partial(local, mesh.shape["space"], mesh.shape["tm"]),
        mesh=mesh,
        in_specs=placed,
        out_specs=(
            P(("rep", "tm"), "space", None, None),
            P(None, None, None, ("rep", "tm"), "space"),
        ),
        check_vma=False,
    )
```

```python
import functools
import math

import jax
import jax.numpy as jnp
from jax import lax
from jax.experimental import pallas as pl
from jax.experimental.pallas import tpu as pltpu
from jax.sharding import PartitionSpec as P

MESH = pl.DeviceIdType.MESH
LANES = 128


def passed_along(array, axis, by):
    length = lax.axis_size(axis)
    pairs = [(i, i + by) for i in range(length) if 0 <= i + by < length]
    return lax.ppermute(array, axis, pairs)


def extended_2(cells, sides, width):
    for axis, dim in sides:
        count = lax.axis_size(axis)
        ends = count - 1
        head = lax.slice_in_dim(cells, 0, width, axis=dim)
        tail = lax.slice_in_dim(cells, cells.shape[dim] - width, cells.shape[dim], axis=dim)
        cells = jnp.concatenate(
            [
                lax.ppermute(tail, axis, [(i, (i + 1) % count) for i in range(ends)]),
                cells,
                lax.ppermute(head, axis, [((i + 1) % count, i) for i in range(ends)]),
            ],
            axis=dim,
        )
    return cells


def reduced(inputs, cotangent, weight):
    frame_count, row_count, col_count, in_channels = inputs.shape
    out_channels = cotangent.shape[3]
    cell_count = frame_count * row_count * col_count
    space_size = lax.axis_size("space")
    time_size = lax.axis_size("tm")
    factor = 1.0 / math.sqrt(cell_count * space_size * time_size)
    earlier = passed_along(inputs, "tm", 1)
    extended = jnp.concatenate([earlier, inputs], axis=0)
    rimmed = extended_2(extended, (("space", 1),), 1)
    padded = jnp.pad(rimmed, ((0, 0), (0, 0), (1, 1), (0, 0)))
    outputs = jnp.zeros((cell_count, out_channels), jnp.float32)
    for depth_tap in range(3):
        for row_tap in range(3):
            for col_tap in range(3):
                window = padded[
                    depth_tap : depth_tap + frame_count,
                    row_tap : row_tap + row_count,
                    col_tap : col_tap + col_count,
                ].reshape(cell_count, in_channels)
                outputs = outputs + jnp.dot(
                    window, weight[depth_tap, row_tap, col_tap], preferred_element_type=jnp.float32
                )
    logistic = jax.nn.sigmoid(outputs)
    derivative = logistic * (1.0 + outputs * (1.0 - logistic))
    upstream = (
        cotangent.reshape(cell_count, out_channels).astype(jnp.float32) * derivative
    ).astype(jnp.bfloat16)
    upstream_grid = upstream.reshape(frame_count, row_count, col_count, out_channels)
    arriving = passed_along(upstream_grid, "tm", -1)
    following = jnp.concatenate([upstream_grid, arriving], axis=0)
    following = extended_2(following, (("space", 1),), 1)
    following = jnp.pad(following, ((0, 0), (0, 0), (1, 1), (0, 0)))
    input_grad = jnp.zeros((cell_count, in_channels), jnp.float32)
    tap_grads = []
    for depth_tap in range(3):
        for row_tap in range(3):
            for col_tap in range(3):
                returned = following[
                    2 - depth_tap : 2 - depth_tap + frame_count,
                    2 - row_tap : 2 - row_tap + row_count,
                    2 - col_tap : 2 - col_tap + col_count,
                ].reshape(cell_count, out_channels)
                input_grad = input_grad + lax.dot_general(
                    returned,
                    weight[depth_tap, row_tap, col_tap],
                    (((1,), (1,)), ((), ())),
                    preferred_element_type=jnp.float32,
                )
                window = padded[
                    depth_tap : depth_tap + frame_count,
                    row_tap : row_tap + row_count,
                    col_tap : col_tap + col_count,
                ].reshape(cell_count, in_channels)
                tap_grads.append(
                    lax.dot_general(
                        window,
                        upstream,
                        (((0,), (0,)), ((), ())),
                        preferred_element_type=jnp.float32,
                    )
                )
    partial_grad = jnp.stack(tap_grads) * factor
    in_share = in_channels // time_size
    out_share = out_channels // space_size
    blocks = partial_grad.reshape(27, in_channels, space_size, out_share)
    blocks = blocks.transpose(2, 0, 1, 3).reshape(space_size * 27, in_channels, out_share)
    spatial_sum = lax.psum_scatter(blocks, "space", scatter_dimension=0, tiled=True)
    blocks = spatial_sum.reshape(27, time_size, in_share, out_share)
    blocks = blocks.transpose(1, 0, 2, 3).reshape(time_size * 27, in_share, out_share)
    owned_part = lax.psum_scatter(blocks, "tm", scatter_dimension=0, tiled=True)
    input_grad = input_grad.reshape(frame_count, row_count, col_count, in_channels).astype(
        jnp.bfloat16
    )
    return (input_grad, owned_part.reshape(3, 3, 3, in_share, out_share))


def shifted_rows(values, by, width):
    count = values.shape[0]
    rows = lax.broadcasted_iota(jnp.int32, values.shape, 0)
    edge = 0 if by < 0 else width - 1
    outside = rows == edge
    for frame in range(1, count // width):
        outside = outside | (rows == frame * width + edge)
    moved = pltpu.roll(values, 1 if by < 0 else count - 1, 0)
    return jnp.where(outside, 0.0, moved)


def transposed_slices(values, width, share, store):
    frames = values.shape[0] // width
    channels = values.shape[1]
    for frame in range(frames):
        part = values[frame * width : (frame + 1) * width]
        part = jnp.concatenate([part, jnp.zeros((LANES - width, channels), part.dtype)], axis=0)
        turned = part.T.astype(jnp.bfloat16)
        for piece in range(channels // share):
            store(piece, frame * share, turned[piece * share : (piece + 1) * share])


def kernel(
    space, time, width, factor,
    x_ref, g_ref, w_hbm, ig_ref, wg_ref,
    w_ref, xbuf, ubuf, xpack, upack, xheld, uheld, xts, uts, xrecv, urecv, xb,
    w_sem, hx_send, hx_recv, hu_send, hu_recv,
    x1_send, x1_recv, up_send, up_recv, down_send, down_recv, u1_send, u1_recv, u2_send, u2_recv,
):
    z = lax.axis_index("space")
    t = lax.axis_index("tm")
    cells, cin = x_ref.shape
    cout = g_ref.shape[1]
    in_share, out_share = cin // time, cout // space
    frames = cells // width
    lanes = space * LANES
    weight_copy = pltpu.make_async_copy(w_hbm, w_ref, w_sem)
    weight_copy.start()

    below, above = z > 0, z < space - 1
    early, late = t > 0, t < time - 1
    partner = t + 1 - 2 * lax.rem(t, 2)

    def at(dz, dt):
        return {"space": z + dz, "tm": t + dt}

    barrier = pltpu.get_barrier_semaphore()
    for step in range(1, space):
        pl.semaphore_signal(
            barrier, 1, device_id={"space": lax.rem(z + step, space), "tm": t}, device_id_type=MESH
        )
    for step in range(1, time):
        pl.semaphore_signal(
            barrier, 1, device_id={"space": z, "tm": lax.rem(t + step, time)}, device_id_type=MESH
        )
    for there, dz, dt in (
        (below & early, -1, -1), (below & late, -1, 1), (above & early, 1, -1), (above & late, 1, 1),
    ):
        @pl.when(there)
        def _(dz=dz, dt=dt):
            pl.semaphore_signal(barrier, 1, device_id=at(dz, dt), device_id_type=MESH)

    def side_by_side(values):
        return jnp.concatenate([values[n * width : (n + 1) * width] for n in range(frames)], axis=1)

    own = x_ref[...]
    xpack[...] = side_by_side(own)
    xbuf[1, cells:] = own

    def keep_x(piece, row, block):
        xts[piece, pl.ds(row, in_share)] = block

    transposed_slices(own.astype(jnp.float32), width, in_share, keep_x)
    xrecv[z, t] = xts[t]
    urecv[:, time * lanes :] = jnp.zeros((frames * out_share, lanes), jnp.bfloat16)
    nothing = jnp.zeros((frames * in_share, LANES), jnp.bfloat16)
    for pair_at in range(time):
        for col in range(3):
            xb[col, :, pair_at * lanes : pair_at * lanes + LANES] = nothing
            xb[6 + col, :, (pair_at + 1) * lanes - LANES : (pair_at + 1) * lanes] = nothing

    @pl.when(jnp.logical_not(early))
    def _():
        for row in range(3):
            xbuf[row, :cells] = jnp.zeros((cells, cin), jnp.bfloat16)

    @pl.when(jnp.logical_not(late))
    def _():
        for row in range(3):
            ubuf[row, cells:] = jnp.zeros((cells, cout), jnp.bfloat16)

    for missing, row in ((jnp.logical_not(below), 0), (jnp.logical_not(above), 2)):
        @pl.when(missing)
        def _(row=row):
            xbuf[row] = jnp.zeros((2 * cells, cin), jnp.bfloat16)
            ubuf[row] = jnp.zeros((2 * cells, cout), jnp.bfloat16)

    beside = (z + space - 1) // space + (2 * space - 2 - z) // space
    around = (t + time - 1) // time + (2 * time - 2 - t) // time
    pl.semaphore_wait(barrier, space + time - 2 + beside * around)

    def remote(source, target, send, recv, slot, device):
        return pltpu.make_async_remote_copy(
            src_ref=source, dst_ref=target, send_sem=send.at[slot], recv_sem=recv.at[slot],
            device_id=device, device_id_type=MESH,
        )

    def halos(pack, held, send, recv, ahead, there, here):
        cases = (
            (0, ahead, there, here),
            (1, 0, above, below),
            (-1, 0, below, above),
            (1, ahead, above & there, below & here),
            (-1, ahead, below & there, above & here),
        )
        return [
            (sent, got, 1 - dz, dt != 0,
             remote(pack, held.at[slot], send, recv, slot, at(dz, dt)))
            for slot, (dz, dt, sent, got) in enumerate(cases)
        ]

    def start_if(there, copy):
        @pl.when(there)
        def _():
            copy.start()

    def unpacked(halo, held, slot, buf, own_half):
        _, got, row, other_time, copy = halo
        half = 1 - own_half if other_time else own_half
        channels = buf.shape[2]

        @pl.when(got)
        def _():
            copy.wait_recv()
            for n in range(frames):
                place = half * cells + n * width
                buf[row, place : place + width] = held[slot, :, n * channels : (n + 1) * channels]

    x_halo = halos(xpack, xheld, hx_send, hx_recv, 1, late, early)
    for sent, _, _, _, copy in x_halo:
        start_if(sent, copy)

    x1, u1 = [], []
    for step in range(1, time):
        other = lax.rem(t + step, time)
        x1.append(remote(xts.at[other], xrecv.at[z, t], x1_send, x1_recv, step - 1,
                         {"space": z, "tm": other}))
    for step in range(1, space):
        other = lax.rem(z + step, space)
        window = urecv.at[:, pl.ds(pl.multiple_of(t * lanes + z * LANES, LANES), LANES)]
        u1.append(remote(uts.at[other], window, u1_send, u1_recv, step - 1,
                         {"space": other, "tm": t}))
    for copy in x1:
        copy.start()

    hops = []
    for step in range(space - 1):
        up, down = xrecv.at[z - step], xrecv.at[z + step]
        hops.append((
            (above & (z >= step), below & (z > step), z - 1 - step,
             remote(up, up, up_send, up_recv, step, at(1, 0))),
            (below & (z + step < space), above & (z + step + 1 < space), z + 1 + step,
             remote(down, down, down_send, down_recv, step, at(-1, 0))),
        ))

    def gather(source_time, slot, device_time):
        window = urecv.at[:, pl.ds(pl.multiple_of(source_time * lanes, LANES), lanes)]
        return remote(window, window, u2_send, u2_recv, slot, {"space": z, "tm": device_time})

    couples = time // 2
    first, second = [gather(t, 0, partner)], []
    for step in range(1, couples):
        first.append(gather(t, step, lax.rem(t + 2 * step, time)))
        came_from = lax.rem(t + time - 2 * step, time)
        second.append(gather(came_from, couples + step - 1, partner))

    def taps(buf, row, depths, forward, totals):
        tap_row = row if forward else 2 - row
        for depth in depths:
            offset = (depth if forward else 2 - depth) * width
            window = buf[row, offset : offset + cells]
            for col in range(3):
                tap = w_ref[(depth * 3 + tap_row) * 3 + col]
                product = lax.dot_general(
                    window, tap, (((1,), (0 if forward else 1,)), ((), ())),
                    preferred_element_type=jnp.float32,
                )
                totals[col] = product if totals[col] is None else totals[col] + product

    def placed(row):
        for pair_at in range(time):
            held = xrecv[row, pair_at]
            wide = held.astype(jnp.float32)
            moved = (
                pltpu.roll(wide, 1, 1).astype(jnp.bfloat16),
                held,
                pltpu.roll(wide, LANES - 1, 1).astype(jnp.bfloat16),
            )
            for tap_row in range(3):
                place = row - tap_row + 1

                @pl.when((place >= 0) & (place < space))
                def _(tap_row=tap_row, place=place):
                    start = pl.multiple_of(pair_at * lanes + place * LANES, LANES)
                    for col in range(3):
                        xb[tap_row * 3 + col, :, pl.ds(start, LANES)] = moved[col]

    def hop_received(step):
        for _, got, _, copy in hops[step]:
            @pl.when(got)
            def _(copy=copy):
                copy.wait_recv()

    def hop_placed(step):
        for _, got, row, _ in hops[step]:
            @pl.when(got)
            def _(row=row):
                placed(row)

    weight_copy.wait()
    sums = [None, None, None]
    taps(xbuf, 1, (2,), True, sums)
    unpacked(x_halo[0], xheld, 0, xbuf, 1)
    taps(xbuf, 1, (0, 1), True, sums)
    unpacked(x_halo[1], xheld, 1, xbuf, 1)
    taps(xbuf, 0, (2,), True, sums)
    unpacked(x_halo[2], xheld, 2, xbuf, 1)
    taps(xbuf, 2, (2,), True, sums)
    unpacked(x_halo[3], xheld, 3, xbuf, 1)
    taps(xbuf, 0, (0, 1), True, sums)
    unpacked(x_halo[4], xheld, 4, xbuf, 1)
    for copy in x1:
        copy.wait_recv()
    for sent, _, _, copy in hops[0]:
        start_if(sent, copy)
    taps(xbuf, 2, (0, 1), True, sums)
    outputs = shifted_rows(sums[0], -1, width) + sums[1] + shifted_rows(sums[2], 1, width)
    logistic = jax.nn.sigmoid(outputs)
    derivative = logistic * (1.0 + outputs * (1.0 - logistic))
    upstream = (g_ref[...].astype(jnp.float32) * derivative).astype(jnp.bfloat16)

    def keep_u(piece, row, block):
        uts[piece, pl.ds(row, out_share)] = block

    transposed_slices(upstream.astype(jnp.float32), width, out_share, keep_u)
    upack[...] = side_by_side(upstream)
    for copy in u1:
        copy.start()
    u_halo = halos(upack, uheld, hu_send, hu_recv, -1, early, late)
    for sent, _, _, _, copy in u_halo:
        start_if(sent, copy)
    ubuf[1, :cells] = upstream
    urecv[:, pl.ds(pl.multiple_of(t * lanes + z * LANES, LANES), LANES)] = uts[z]
    hop_received(0)
    if space > 2:
        for sent, _, _, copy in hops[1]:
            start_if(sent, copy)
    placed(z)
    hop_placed(0)

    for copy in u1:
        copy.wait_recv()
    for copy in first:
        copy.start()

    for step in range(1, space - 1):
        hop_received(step)
        if step + 1 < space - 1:
            for sent, _, _, copy in hops[step + 1]:
                start_if(sent, copy)
        if step + 1 < space - 1:
            hop_placed(step)

    sums = [None, None, None]
    taps(ubuf, 1, (2,), False, sums)
    unpacked(u_halo[0], uheld, 0, ubuf, 0)
    taps(ubuf, 1, (0, 1), False, sums)
    unpacked(u_halo[1], uheld, 1, ubuf, 0)
    taps(ubuf, 0, (2,), False, sums)
    unpacked(u_halo[2], uheld, 2, ubuf, 0)
    taps(ubuf, 2, (2,), False, sums)
    for copy in first[1:]:
        copy.wait_recv()
    for copy in second:
        copy.start()
    unpacked(u_halo[3], uheld, 3, ubuf, 0)
    taps(ubuf, 0, (0, 1), False, sums)
    unpacked(u_halo[4], uheld, 4, ubuf, 0)
    taps(ubuf, 2, (0, 1), False, sums)
    total = shifted_rows(sums[0], 1, width) + sums[1] + shifted_rows(sums[2], -1, width)
    ig_ref[...] = total.astype(jnp.bfloat16)
    if space > 2:
        hop_placed(space - 2)

    first[0].wait_recv()
    for copy in second:
        copy.wait_recv()
    both = jnp.concatenate([urecv[:, : time * lanes], urecv[:, lanes:]], axis=0)
    for tap_row in range(3):
        left = xb[tap_row * 3 : tap_row * 3 + 3].reshape(3 * frames * in_share, time * lanes)
        grads = lax.dot_general(
            left, both, (((1,), (1,)), ((), ())), preferred_element_type=jnp.float32
        ) * factor
        grads = grads.reshape(3, frames, in_share, 2 * frames * out_share)
        for col in range(3):
            joined = grads[col, 0, :, : 3 * out_share] + grads[col, 1, :, out_share:]
            for depth in range(3):
                lag = 2 - depth
                wg_ref[(depth * 3 + tap_row) * 3 + col] = joined[:, lag * out_share : (lag + 1) * out_share]

    for copy in x1 + u1 + first + second:
        copy.wait_send()
    for sent, _, _, _, copy in x_halo + u_halo:
        @pl.when(sent)
        def _(copy=copy):
            copy.wait_send()
    for pair in hops:
        for sent, _, _, copy in pair:
            @pl.when(sent)
            def _(copy=copy):
                copy.wait_send()


def written(ig_ref, wg_ref, ig_out, wg_out, sems):
    copies = [
        pltpu.make_async_copy(wg_ref, wg_out, sems.at[0]),
        pltpu.make_async_copy(ig_ref, ig_out, sems.at[1]),
    ]
    for copy in copies:
        copy.start()
    for copy in copies:
        copy.wait()


def gathered(space, time, inputs, cotangent, weight):
    frames, _, width, cin = inputs.shape
    cout = cotangent.shape[3]
    cells = frames * width
    in_share, out_share = cin // time, cout // space
    lanes = space * LANES
    factor = 1.0 / math.sqrt(cells * space * time)
    vmem = pl.BlockSpec(memory_space=pltpu.VMEM)
    dma = pltpu.SemaphoreType.DMA
    bf16 = jnp.bfloat16
    input_grad, weight_grad = pl.pallas_call(
        functools.partial(kernel, space, time, width, factor),
        out_shape=(
            jax.ShapeDtypeStruct((cells, cin), bf16),
            jax.ShapeDtypeStruct((27, in_share, out_share), jnp.float32),
        ),
        in_specs=[vmem, vmem, pl.BlockSpec(memory_space=pl.ANY)],
        out_specs=(vmem, vmem),
        scratch_shapes=[
            pltpu.VMEM((27, cin, cout), bf16),
            pltpu.VMEM((3, 2 * cells, cin), bf16),
            pltpu.VMEM((3, 2 * cells, cout), bf16),
            pltpu.VMEM((width, frames * cin), bf16),
            pltpu.VMEM((width, frames * cout), bf16),
            pltpu.VMEM((5, width, frames * cin), bf16),
            pltpu.VMEM((5, width, frames * cout), bf16),
            pltpu.VMEM((time, frames * in_share, LANES), bf16),
            pltpu.VMEM((space, frames * out_share, LANES), bf16),
            pltpu.VMEM((space, time, frames * in_share, LANES), bf16),
            pltpu.VMEM((frames * out_share, (time + 1) * lanes), bf16),
            pltpu.VMEM((9, frames * in_share, time * lanes), bf16),
            dma,
            dma((5,)), dma((5,)), dma((5,)), dma((5,)),
            dma((time - 1,)), dma((time - 1,)),
            dma((space - 1,)), dma((space - 1,)), dma((space - 1,)), dma((space - 1,)),
            dma((space - 1,)), dma((space - 1,)), dma((time - 1,)), dma((time - 1,)),
        ],
        compiler_params=pltpu.CompilerParams(
            collective_id=0, has_side_effects=True, vmem_limit_bytes=62 * 1024 * 1024
        ),
    )(inputs.reshape(cells, cin), cotangent.reshape(cells, cout), weight.reshape(27, cin, cout))
    anywhere = pl.BlockSpec(memory_space=pl.ANY)
    input_grad, weight_grad = pl.pallas_call(
        written,
        out_shape=(
            jax.ShapeDtypeStruct(input_grad.shape, bf16),
            jax.ShapeDtypeStruct(weight_grad.shape, jnp.float32),
        ),
        in_specs=[vmem, vmem],
        out_specs=(anywhere, anywhere),
        scratch_shapes=[dma((2,))],
    )(input_grad, weight_grad)
    return (
        input_grad.reshape(inputs.shape),
        weight_grad.reshape(3, 3, 3, in_share, out_share),
    )


def local(space, time, inputs, cotangent, weight):
    frames, rows, width, cin = inputs.shape
    cout = cotangent.shape[3]
    slices = 2 * frames * rows * width * space * time * (cin // time + cout // space)
    partials = 4 * 27 * cin * cout
    fits = (
        frames == 2
        and rows == 1
        and width < LANES
        and width % 16 == 0
        and space > 1
        and time % 2 == 0
        and (cin // time) % 16 == 0
        and (cout // space) % 16 == 0
    )
    if fits and slices < partials:
        return gathered(space, time, inputs, cotangent, weight)
    return reduced(inputs, cotangent, weight)


def solution(mesh):
    placed = (P(("rep", "tm"), "space", None, None), P(("rep", "tm"), "space", None, None), P())
    return jax.shard_map(
        functools.partial(local, mesh.shape["space"], mesh.shape["tm"]),
        mesh=mesh,
        in_specs=placed,
        out_specs=(
            P(("rep", "tm"), "space", None, None),
            P(None, None, None, ("rep", "tm"), "space"),
        ),
        check_vma=False,
    )
```

```python
import functools
import math

import jax
import jax.numpy as jnp
from jax import lax
from jax.experimental import pallas as pl
from jax.experimental.pallas import tpu as pltpu
from jax.sharding import PartitionSpec as P

MESH = pl.DeviceIdType.MESH
LANES = 128


def passed_along(array, axis, by):
    length = lax.axis_size(axis)
    pairs = [(i, i + by) for i in range(length) if 0 <= i + by < length]
    return lax.ppermute(array, axis, pairs)


def extended_2(cells, sides, width):
    for axis, dim in sides:
        count = lax.axis_size(axis)
        ends = count - 1
        head = lax.slice_in_dim(cells, 0, width, axis=dim)
        tail = lax.slice_in_dim(cells, cells.shape[dim] - width, cells.shape[dim], axis=dim)
        cells = jnp.concatenate(
            [
                lax.ppermute(tail, axis, [(i, (i + 1) % count) for i in range(ends)]),
                cells,
                lax.ppermute(head, axis, [((i + 1) % count, i) for i in range(ends)]),
            ],
            axis=dim,
        )
    return cells


def reduced(inputs, cotangent, weight):
    frame_count, row_count, col_count, in_channels = inputs.shape
    out_channels = cotangent.shape[3]
    cell_count = frame_count * row_count * col_count
    space_size = lax.axis_size("space")
    time_size = lax.axis_size("tm")
    factor = 1.0 / math.sqrt(cell_count * space_size * time_size)
    earlier = passed_along(inputs, "tm", 1)
    extended = jnp.concatenate([earlier, inputs], axis=0)
    rimmed = extended_2(extended, (("space", 1),), 1)
    padded = jnp.pad(rimmed, ((0, 0), (0, 0), (1, 1), (0, 0)))
    outputs = jnp.zeros((cell_count, out_channels), jnp.float32)
    for depth_tap in range(3):
        for row_tap in range(3):
            for col_tap in range(3):
                window = padded[
                    depth_tap : depth_tap + frame_count,
                    row_tap : row_tap + row_count,
                    col_tap : col_tap + col_count,
                ].reshape(cell_count, in_channels)
                outputs = outputs + jnp.dot(
                    window, weight[depth_tap, row_tap, col_tap], preferred_element_type=jnp.float32
                )
    logistic = jax.nn.sigmoid(outputs)
    derivative = logistic * (1.0 + outputs * (1.0 - logistic))
    upstream = (
        cotangent.reshape(cell_count, out_channels).astype(jnp.float32) * derivative
    ).astype(jnp.bfloat16)
    upstream_grid = upstream.reshape(frame_count, row_count, col_count, out_channels)
    arriving = passed_along(upstream_grid, "tm", -1)
    following = jnp.concatenate([upstream_grid, arriving], axis=0)
    following = extended_2(following, (("space", 1),), 1)
    following = jnp.pad(following, ((0, 0), (0, 0), (1, 1), (0, 0)))
    input_grad = jnp.zeros((cell_count, in_channels), jnp.float32)
    tap_grads = []
    for depth_tap in range(3):
        for row_tap in range(3):
            for col_tap in range(3):
                returned = following[
                    2 - depth_tap : 2 - depth_tap + frame_count,
                    2 - row_tap : 2 - row_tap + row_count,
                    2 - col_tap : 2 - col_tap + col_count,
                ].reshape(cell_count, out_channels)
                input_grad = input_grad + lax.dot_general(
                    returned,
                    weight[depth_tap, row_tap, col_tap],
                    (((1,), (1,)), ((), ())),
                    preferred_element_type=jnp.float32,
                )
                window = padded[
                    depth_tap : depth_tap + frame_count,
                    row_tap : row_tap + row_count,
                    col_tap : col_tap + col_count,
                ].reshape(cell_count, in_channels)
                tap_grads.append(
                    lax.dot_general(
                        window,
                        upstream,
                        (((0,), (0,)), ((), ())),
                        preferred_element_type=jnp.float32,
                    )
                )
    partial_grad = jnp.stack(tap_grads) * factor
    in_share = in_channels // time_size
    out_share = out_channels // space_size
    blocks = partial_grad.reshape(27, in_channels, space_size, out_share)
    blocks = blocks.transpose(2, 0, 1, 3).reshape(space_size * 27, in_channels, out_share)
    spatial_sum = lax.psum_scatter(blocks, "space", scatter_dimension=0, tiled=True)
    blocks = spatial_sum.reshape(27, time_size, in_share, out_share)
    blocks = blocks.transpose(1, 0, 2, 3).reshape(time_size * 27, in_share, out_share)
    owned_part = lax.psum_scatter(blocks, "tm", scatter_dimension=0, tiled=True)
    input_grad = input_grad.reshape(frame_count, row_count, col_count, in_channels).astype(
        jnp.bfloat16
    )
    return (input_grad, owned_part.reshape(3, 3, 3, in_share, out_share))


def shifted_rows(values, by, width):
    count = values.shape[0]
    rows = lax.broadcasted_iota(jnp.int32, values.shape, 0)
    edge = 0 if by < 0 else width - 1
    outside = rows == edge
    for frame in range(1, count // width):
        outside = outside | (rows == frame * width + edge)
    moved = pltpu.roll(values, 1 if by < 0 else count - 1, 0)
    return jnp.where(outside, 0.0, moved)


def transposed_slices(values, width, share, store):
    frames = values.shape[0] // width
    channels = values.shape[1]
    for frame in range(frames):
        part = values[frame * width : (frame + 1) * width]
        part = jnp.concatenate([part, jnp.zeros((LANES - width, channels), part.dtype)], axis=0)
        turned = part.T.astype(jnp.bfloat16)
        for piece in range(channels // share):
            store(piece, frame * share, turned[piece * share : (piece + 1) * share])


def kernel(
    space, time, width, factor,
    x_hbm, g_hbm, w_hbm, ig_ref, wg_ref,
    x_ref, g_ref, w_ref, xbuf, ubuf, xpack, upack, xheld, uheld, xts, uts, xrecv, urecv, xb,
    load_sem, hx_send, hx_recv, hu_send, hu_recv,
    x1_send, x1_recv, up_send, up_recv, down_send, down_recv, u1_send, u1_recv, u2_send, u2_recv,
):
    z = lax.axis_index("space")
    t = lax.axis_index("tm")
    cells, cin = x_ref.shape
    cout = g_ref.shape[1]
    in_share, out_share = cin // time, cout // space
    frames = cells // width
    lanes = space * LANES
    input_copy = pltpu.make_async_copy(x_hbm, x_ref, load_sem.at[0])
    weight_copy = pltpu.make_async_copy(w_hbm, w_ref, load_sem.at[1])
    cotangent_copy = pltpu.make_async_copy(g_hbm, g_ref, load_sem.at[2])
    for copy in (input_copy, weight_copy, cotangent_copy):
        copy.start()

    below, above = z > 0, z < space - 1
    early, late = t > 0, t < time - 1
    partner = t + 1 - 2 * lax.rem(t, 2)

    def at(dz, dt):
        return {"space": z + dz, "tm": t + dt}

    barrier = pltpu.get_barrier_semaphore()
    for step in range(1, space):
        pl.semaphore_signal(
            barrier, 1, device_id={"space": lax.rem(z + step, space), "tm": t}, device_id_type=MESH
        )
    for step in range(1, time):
        pl.semaphore_signal(
            barrier, 1, device_id={"space": z, "tm": lax.rem(t + step, time)}, device_id_type=MESH
        )
    for there, dz, dt in (
        (below & early, -1, -1), (below & late, -1, 1), (above & early, 1, -1), (above & late, 1, 1),
    ):
        @pl.when(there)
        def _(dz=dz, dt=dt):
            pl.semaphore_signal(barrier, 1, device_id=at(dz, dt), device_id_type=MESH)

    def side_by_side(values):
        return jnp.concatenate([values[n * width : (n + 1) * width] for n in range(frames)], axis=1)

    input_copy.wait()
    own = x_ref[...]
    xpack[...] = side_by_side(own)
    xbuf[1, cells:] = own

    def keep_x(piece, row, block):
        xts[piece, pl.ds(row, in_share)] = block

    transposed_slices(own.astype(jnp.float32), width, in_share, keep_x)
    xrecv[z, t] = xts[t]
    urecv[:, time * lanes :] = jnp.zeros((frames * out_share, lanes), jnp.bfloat16)
    nothing = jnp.zeros((frames * in_share, LANES), jnp.bfloat16)
    for pair_at in range(time):
        for col in range(3):
            xb[col, :, pair_at * lanes : pair_at * lanes + LANES] = nothing
            xb[6 + col, :, (pair_at + 1) * lanes - LANES : (pair_at + 1) * lanes] = nothing

    @pl.when(jnp.logical_not(early))
    def _():
        for row in range(3):
            xbuf[row, :cells] = jnp.zeros((cells, cin), jnp.bfloat16)

    @pl.when(jnp.logical_not(late))
    def _():
        for row in range(3):
            ubuf[row, cells:] = jnp.zeros((cells, cout), jnp.bfloat16)

    for missing, row in ((jnp.logical_not(below), 0), (jnp.logical_not(above), 2)):
        @pl.when(missing)
        def _(row=row):
            xbuf[row] = jnp.zeros((2 * cells, cin), jnp.bfloat16)
            ubuf[row] = jnp.zeros((2 * cells, cout), jnp.bfloat16)

    beside = (z + space - 1) // space + (2 * space - 2 - z) // space
    around = (t + time - 1) // time + (2 * time - 2 - t) // time
    pl.semaphore_wait(barrier, space + time - 2 + beside * around)

    def remote(source, target, send, recv, slot, device):
        return pltpu.make_async_remote_copy(
            src_ref=source, dst_ref=target, send_sem=send.at[slot], recv_sem=recv.at[slot],
            device_id=device, device_id_type=MESH,
        )

    def halos(pack, held, send, recv, ahead, there, here):
        cases = (
            (0, ahead, there, here),
            (1, 0, above, below),
            (-1, 0, below, above),
            (1, ahead, above & there, below & here),
            (-1, ahead, below & there, above & here),
        )
        return [
            (sent, got, 1 - dz, dt != 0,
             remote(pack, held.at[slot], send, recv, slot, at(dz, dt)))
            for slot, (dz, dt, sent, got) in enumerate(cases)
        ]

    def start_if(there, copy):
        @pl.when(there)
        def _():
            copy.start()

    def unpacked(halo, held, slot, buf, own_half):
        _, got, row, other_time, copy = halo
        half = 1 - own_half if other_time else own_half
        channels = buf.shape[2]

        @pl.when(got)
        def _():
            copy.wait_recv()
            for n in range(frames):
                place = half * cells + n * width
                buf[row, place : place + width] = held[slot, :, n * channels : (n + 1) * channels]

    x_halo = halos(xpack, xheld, hx_send, hx_recv, 1, late, early)
    for sent, _, _, _, copy in x_halo:
        start_if(sent, copy)

    x1, u1 = [], []
    for step in range(1, time):
        other = lax.rem(t + step, time)
        x1.append(remote(xts.at[other], xrecv.at[z, t], x1_send, x1_recv, step - 1,
                         {"space": z, "tm": other}))
    for step in range(1, space):
        other = lax.rem(z + step, space)
        window = urecv.at[:, pl.ds(pl.multiple_of(t * lanes + z * LANES, LANES), LANES)]
        u1.append(remote(uts.at[other], window, u1_send, u1_recv, step - 1,
                         {"space": other, "tm": t}))
    for copy in x1:
        copy.start()

    hops = []
    for step in range(space - 1):
        up, down = xrecv.at[z - step], xrecv.at[z + step]
        hops.append((
            (above & (z >= step), below & (z > step), z - 1 - step,
             remote(up, up, up_send, up_recv, step, at(1, 0))),
            (below & (z + step < space), above & (z + step + 1 < space), z + 1 + step,
             remote(down, down, down_send, down_recv, step, at(-1, 0))),
        ))

    couples = time // 2

    def gather(piece, source_time, slot, device_time):
        row = lax.rem(z + space - piece, space)
        start = pl.multiple_of(source_time * lanes + row * LANES, LANES)
        window = urecv.at[:, pl.ds(start, LANES)]
        return remote(window, window, u2_send, u2_recv, piece * (time - 1) + slot,
                      {"space": z, "tm": device_time})

    first, second = [], []
    for piece in range(space):
        first.append([gather(piece, t, 0, partner)])
        second.append([])
        for step in range(1, couples):
            came_from = lax.rem(t + time - 2 * step, time)
            first[piece].append(gather(piece, t, step, lax.rem(t + 2 * step, time)))
            second[piece].append(gather(piece, came_from, couples + step - 1, partner))

    def handed_on(piece):
        for held, copy in zip(first[piece][1:], second[piece]):
            held.wait_recv()
            copy.start()

    def taps(buf, row, depths, forward, totals):
        tap_row = row if forward else 2 - row
        for depth in depths:
            offset = (depth if forward else 2 - depth) * width
            window = buf[row, offset : offset + cells]
            for col in range(3):
                tap = w_ref[(depth * 3 + tap_row) * 3 + col]
                product = lax.dot_general(
                    window, tap, (((1,), (0 if forward else 1,)), ((), ())),
                    preferred_element_type=jnp.float32,
                )
                totals[col] = product if totals[col] is None else totals[col] + product

    def placed(row):
        for pair_at in range(time):
            held = xrecv[row, pair_at]
            wide = held.astype(jnp.float32)
            moved = (
                pltpu.roll(wide, 1, 1).astype(jnp.bfloat16),
                held,
                pltpu.roll(wide, LANES - 1, 1).astype(jnp.bfloat16),
            )
            for tap_row in range(3):
                place = row - tap_row + 1

                @pl.when((place >= 0) & (place < space))
                def _(tap_row=tap_row, place=place):
                    start = pl.multiple_of(pair_at * lanes + place * LANES, LANES)
                    for col in range(3):
                        xb[tap_row * 3 + col, :, pl.ds(start, LANES)] = moved[col]

    def hop_received(step):
        for _, got, _, copy in hops[step]:
            @pl.when(got)
            def _(copy=copy):
                copy.wait_recv()

    def hop_placed(step):
        for _, got, row, _ in hops[step]:
            @pl.when(got)
            def _(row=row):
                placed(row)

    weight_copy.wait()
    sums = [None, None, None]
    taps(xbuf, 1, (2,), True, sums)
    unpacked(x_halo[0], xheld, 0, xbuf, 1)
    taps(xbuf, 1, (0, 1), True, sums)
    unpacked(x_halo[1], xheld, 1, xbuf, 1)
    taps(xbuf, 0, (2,), True, sums)
    unpacked(x_halo[2], xheld, 2, xbuf, 1)
    taps(xbuf, 2, (2,), True, sums)
    unpacked(x_halo[3], xheld, 3, xbuf, 1)
    taps(xbuf, 0, (0, 1), True, sums)
    unpacked(x_halo[4], xheld, 4, xbuf, 1)
    for copy in x1:
        copy.wait_recv()
    for sent, _, _, copy in hops[0]:
        start_if(sent, copy)
    taps(xbuf, 2, (0, 1), True, sums)
    outputs = shifted_rows(sums[0], -1, width) + sums[1] + shifted_rows(sums[2], 1, width)
    logistic = jax.nn.sigmoid(outputs)
    derivative = logistic * (1.0 + outputs * (1.0 - logistic))
    cotangent_copy.wait()
    upstream = (g_ref[...].astype(jnp.float32) * derivative).astype(jnp.bfloat16)

    def keep_u(piece, row, block):
        uts[piece, pl.ds(row, out_share)] = block

    transposed_slices(upstream.astype(jnp.float32), width, out_share, keep_u)
    upack[...] = side_by_side(upstream)
    for copy in u1:
        copy.start()
    urecv[:, pl.ds(pl.multiple_of(t * lanes + z * LANES, LANES), LANES)] = uts[z]
    for copy in first[0]:
        copy.start()
    u_halo = halos(upack, uheld, hu_send, hu_recv, -1, early, late)
    for sent, _, _, _, copy in u_halo:
        start_if(sent, copy)
    ubuf[1, :cells] = upstream
    hop_received(0)
    if space > 2:
        for sent, _, _, copy in hops[1]:
            start_if(sent, copy)
    placed(z)
    sums = [None, None, None]
    taps(ubuf, 1, (2,), False, sums)

    for step in range(1, space):
        u1[step - 1].wait_recv()
        for copy in first[step]:
            copy.start()
    hop_placed(0)
    for step in range(1, space - 1):
        hop_received(step)
        if step + 1 < space - 1:
            for sent, _, _, copy in hops[step + 1]:
                start_if(sent, copy)
    handed_on(0)
    unpacked(u_halo[0], uheld, 0, ubuf, 0)
    taps(ubuf, 1, (0, 1), False, sums)
    for piece in range(1, space - 1):
        handed_on(piece)
    unpacked(u_halo[1], uheld, 1, ubuf, 0)
    taps(ubuf, 0, (2,), False, sums)
    handed_on(space - 1)
    unpacked(u_halo[2], uheld, 2, ubuf, 0)
    taps(ubuf, 2, (2,), False, sums)
    unpacked(u_halo[3], uheld, 3, ubuf, 0)
    taps(ubuf, 0, (0, 1), False, sums)
    unpacked(u_halo[4], uheld, 4, ubuf, 0)
    taps(ubuf, 2, (0, 1), False, sums)
    total = shifted_rows(sums[0], 1, width) + sums[1] + shifted_rows(sums[2], -1, width)
    ig_ref[...] = total.astype(jnp.bfloat16)
    for step in range(1, space - 1):
        hop_placed(step)

    for piece in range(space):
        first[piece][0].wait_recv()
        for copy in second[piece]:
            copy.wait_recv()
    both = jnp.concatenate([urecv[:, : time * lanes], urecv[:, lanes:]], axis=0)
    for tap_row in range(3):
        left = xb[tap_row * 3 : tap_row * 3 + 3].reshape(3 * frames * in_share, time * lanes)
        grads = lax.dot_general(
            left, both, (((1,), (1,)), ((), ())), preferred_element_type=jnp.float32
        ) * factor
        grads = grads.reshape(3, frames, in_share, 2 * frames * out_share)
        for col in range(3):
            joined = grads[col, 0, :, : 3 * out_share] + grads[col, 1, :, out_share:]
            for depth in range(3):
                lag = 2 - depth
                wg_ref[(depth * 3 + tap_row) * 3 + col] = joined[:, lag * out_share : (lag + 1) * out_share]

    for copy in x1 + u1 + sum(first, []) + sum(second, []):
        copy.wait_send()
    for sent, _, _, _, copy in x_halo + u_halo:
        @pl.when(sent)
        def _(copy=copy):
            copy.wait_send()
    for pair in hops:
        for sent, _, _, copy in pair:
            @pl.when(sent)
            def _(copy=copy):
                copy.wait_send()


def written(ig_ref, wg_ref, ig_out, wg_out, sems):
    copies = [
        pltpu.make_async_copy(wg_ref, wg_out, sems.at[0]),
        pltpu.make_async_copy(ig_ref, ig_out, sems.at[1]),
    ]
    for copy in copies:
        copy.start()
    for copy in copies:
        copy.wait()


def gathered(space, time, inputs, cotangent, weight):
    frames, _, width, cin = inputs.shape
    cout = cotangent.shape[3]
    cells = frames * width
    in_share, out_share = cin // time, cout // space
    lanes = space * LANES
    factor = 1.0 / math.sqrt(cells * space * time)
    vmem = pl.BlockSpec(memory_space=pltpu.VMEM)
    hbm = pl.BlockSpec(memory_space=pltpu.HBM)
    dma = pltpu.SemaphoreType.DMA
    bf16 = jnp.bfloat16
    input_grad, weight_grad = pl.pallas_call(
        functools.partial(kernel, space, time, width, factor),
        out_shape=(
            jax.ShapeDtypeStruct((cells, cin), bf16),
            jax.ShapeDtypeStruct((27, in_share, out_share), jnp.float32),
        ),
        in_specs=[hbm, hbm, hbm],
        out_specs=(vmem, vmem),
        scratch_shapes=[
            pltpu.VMEM((cells, cin), bf16),
            pltpu.VMEM((cells, cout), bf16),
            pltpu.VMEM((27, cin, cout), bf16),
            pltpu.VMEM((3, 2 * cells, cin), bf16),
            pltpu.VMEM((3, 2 * cells, cout), bf16),
            pltpu.VMEM((width, frames * cin), bf16),
            pltpu.VMEM((width, frames * cout), bf16),
            pltpu.VMEM((5, width, frames * cin), bf16),
            pltpu.VMEM((5, width, frames * cout), bf16),
            pltpu.VMEM((time, frames * in_share, LANES), bf16),
            pltpu.VMEM((space, frames * out_share, LANES), bf16),
            pltpu.VMEM((space, time, frames * in_share, LANES), bf16),
            pltpu.VMEM((frames * out_share, (time + 1) * lanes), bf16),
            pltpu.VMEM((9, frames * in_share, time * lanes), bf16),
            dma((3,)),
            dma((5,)), dma((5,)), dma((5,)), dma((5,)),
            dma((time - 1,)), dma((time - 1,)),
            dma((space - 1,)), dma((space - 1,)), dma((space - 1,)), dma((space - 1,)),
            dma((space - 1,)), dma((space - 1,)), dma((space * (time - 1),)), dma((space * (time - 1),)),
        ],
        compiler_params=pltpu.CompilerParams(
            collective_id=0, has_side_effects=True, vmem_limit_bytes=52 * 1024 * 1024
        ),
    )(inputs.reshape(cells, cin), cotangent.reshape(cells, cout), weight.reshape(27, cin, cout))
    input_grad, weight_grad = pl.pallas_call(
        written,
        out_shape=(
            jax.ShapeDtypeStruct(input_grad.shape, bf16),
            jax.ShapeDtypeStruct(weight_grad.shape, jnp.float32),
        ),
        in_specs=[vmem, vmem],
        out_specs=(hbm, hbm),
        scratch_shapes=[dma((2,))],
        compiler_params=pltpu.CompilerParams(vmem_limit_bytes=8 * 1024 * 1024),
    )(input_grad, weight_grad)
    return (
        input_grad.reshape(inputs.shape),
        weight_grad.reshape(3, 3, 3, in_share, out_share),
    )


def local(space, time, inputs, cotangent, weight):
    frames, rows, width, cin = inputs.shape
    cout = cotangent.shape[3]
    slices = 2 * frames * rows * width * space * time * (cin // time + cout // space)
    partials = 4 * 27 * cin * cout
    fits = (
        frames == 2
        and rows == 1
        and width < LANES
        and width % 16 == 0
        and space > 1
        and time % 2 == 0
        and (cin // time) % 16 == 0
        and (cout // space) % 16 == 0
    )
    if fits and slices < partials:
        return gathered(space, time, inputs, cotangent, weight)
    return reduced(inputs, cotangent, weight)


def solution(mesh):
    placed = (P(("rep", "tm"), "space", None, None), P(("rep", "tm"), "space", None, None), P())
    return jax.shard_map(
        functools.partial(local, mesh.shape["space"], mesh.shape["tm"]),
        mesh=mesh,
        in_specs=placed,
        out_specs=(
            P(("rep", "tm"), "space", None, None),
            P(None, None, None, ("rep", "tm"), "space"),
        ),
        check_vma=False,
    )
```

```python
import functools
import math

import jax
import jax.numpy as jnp
from jax import lax
from jax.experimental import pallas as pl
from jax.experimental.pallas import tpu as pltpu
from jax.sharding import PartitionSpec as P

MESH = pl.DeviceIdType.MESH
LANES = 128


def passed_along(array, axis, by):
    length = lax.axis_size(axis)
    pairs = [(i, i + by) for i in range(length) if 0 <= i + by < length]
    return lax.ppermute(array, axis, pairs)


def extended_2(cells, sides, width):
    for axis, dim in sides:
        count = lax.axis_size(axis)
        ends = count - 1
        head = lax.slice_in_dim(cells, 0, width, axis=dim)
        tail = lax.slice_in_dim(cells, cells.shape[dim] - width, cells.shape[dim], axis=dim)
        cells = jnp.concatenate(
            [
                lax.ppermute(tail, axis, [(i, (i + 1) % count) for i in range(ends)]),
                cells,
                lax.ppermute(head, axis, [((i + 1) % count, i) for i in range(ends)]),
            ],
            axis=dim,
        )
    return cells


def reduced(inputs, cotangent, weight):
    frame_count, row_count, col_count, in_channels = inputs.shape
    out_channels = cotangent.shape[3]
    cell_count = frame_count * row_count * col_count
    space_size = lax.axis_size("space")
    time_size = lax.axis_size("tm")
    factor = 1.0 / math.sqrt(cell_count * space_size * time_size)
    earlier = passed_along(inputs, "tm", 1)
    extended = jnp.concatenate([earlier, inputs], axis=0)
    rimmed = extended_2(extended, (("space", 1),), 1)
    padded = jnp.pad(rimmed, ((0, 0), (0, 0), (1, 1), (0, 0)))
    outputs = jnp.zeros((cell_count, out_channels), jnp.float32)
    for depth_tap in range(3):
        for row_tap in range(3):
            for col_tap in range(3):
                window = padded[
                    depth_tap : depth_tap + frame_count,
                    row_tap : row_tap + row_count,
                    col_tap : col_tap + col_count,
                ].reshape(cell_count, in_channels)
                outputs = outputs + jnp.dot(
                    window, weight[depth_tap, row_tap, col_tap], preferred_element_type=jnp.float32
                )
    logistic = jax.nn.sigmoid(outputs)
    derivative = logistic * (1.0 + outputs * (1.0 - logistic))
    upstream = (
        cotangent.reshape(cell_count, out_channels).astype(jnp.float32) * derivative
    ).astype(jnp.bfloat16)
    upstream_grid = upstream.reshape(frame_count, row_count, col_count, out_channels)
    arriving = passed_along(upstream_grid, "tm", -1)
    following = jnp.concatenate([upstream_grid, arriving], axis=0)
    following = extended_2(following, (("space", 1),), 1)
    following = jnp.pad(following, ((0, 0), (0, 0), (1, 1), (0, 0)))
    input_grad = jnp.zeros((cell_count, in_channels), jnp.float32)
    tap_grads = []
    for depth_tap in range(3):
        for row_tap in range(3):
            for col_tap in range(3):
                returned = following[
                    2 - depth_tap : 2 - depth_tap + frame_count,
                    2 - row_tap : 2 - row_tap + row_count,
                    2 - col_tap : 2 - col_tap + col_count,
                ].reshape(cell_count, out_channels)
                input_grad = input_grad + lax.dot_general(
                    returned,
                    weight[depth_tap, row_tap, col_tap],
                    (((1,), (1,)), ((), ())),
                    preferred_element_type=jnp.float32,
                )
                window = padded[
                    depth_tap : depth_tap + frame_count,
                    row_tap : row_tap + row_count,
                    col_tap : col_tap + col_count,
                ].reshape(cell_count, in_channels)
                tap_grads.append(
                    lax.dot_general(
                        window,
                        upstream,
                        (((0,), (0,)), ((), ())),
                        preferred_element_type=jnp.float32,
                    )
                )
    partial_grad = jnp.stack(tap_grads) * factor
    in_share = in_channels // time_size
    out_share = out_channels // space_size
    blocks = partial_grad.reshape(27, in_channels, space_size, out_share)
    blocks = blocks.transpose(2, 0, 1, 3).reshape(space_size * 27, in_channels, out_share)
    spatial_sum = lax.psum_scatter(blocks, "space", scatter_dimension=0, tiled=True)
    blocks = spatial_sum.reshape(27, time_size, in_share, out_share)
    blocks = blocks.transpose(1, 0, 2, 3).reshape(time_size * 27, in_share, out_share)
    owned_part = lax.psum_scatter(blocks, "tm", scatter_dimension=0, tiled=True)
    input_grad = input_grad.reshape(frame_count, row_count, col_count, in_channels).astype(
        jnp.bfloat16
    )
    return (input_grad, owned_part.reshape(3, 3, 3, in_share, out_share))


def shifted_rows(values, by, width):
    count = values.shape[0]
    rows = lax.broadcasted_iota(jnp.int32, values.shape, 0)
    edge = 0 if by < 0 else width - 1
    outside = rows == edge
    for frame in range(1, count // width):
        outside = outside | (rows == frame * width + edge)
    moved = pltpu.roll(values, 1 if by < 0 else count - 1, 0)
    return jnp.where(outside, 0.0, moved)


def transposed_slices(values, width, share, store):
    frames = values.shape[0] // width
    channels = values.shape[1]
    for frame in range(frames):
        part = values[frame * width : (frame + 1) * width]
        part = jnp.concatenate([part, jnp.zeros((LANES - width, channels), part.dtype)], axis=0)
        turned = part.T.astype(jnp.bfloat16)
        for piece in range(channels // share):
            store(piece, frame * share, turned[piece * share : (piece + 1) * share])


def kernel(
    space, time, width, factor,
    x_hbm, g_hbm, w_hbm, ig_ref, wg_ref,
    x_ref, g_ref, w_ref, xbuf, ubuf, xpack, upack, xheld, uheld, xts, uts, xrecv, urecv, xb,
    load_sem, hx_send, hx_recv, hu_send, hu_recv,
    x1_send, x1_recv, up_send, up_recv, down_send, down_recv, u1_send, u1_recv, u2_send, u2_recv,
):
    z = lax.axis_index("space")
    t = lax.axis_index("tm")
    cells, cin = x_ref.shape
    cout = g_ref.shape[1]
    in_share, out_share = cin // time, cout // space
    frames = cells // width
    lanes = space * LANES
    input_copy = pltpu.make_async_copy(x_hbm, x_ref, load_sem.at[0])
    weight_copy = pltpu.make_async_copy(w_hbm, w_ref, load_sem.at[1])
    cotangent_copy = pltpu.make_async_copy(g_hbm, g_ref, load_sem.at[2])
    for copy in (input_copy, weight_copy, cotangent_copy):
        copy.start()

    below, above = z > 0, z < space - 1
    early, late = t > 0, t < time - 1
    partner = t + 1 - 2 * lax.rem(t, 2)

    def at(dz, dt):
        return {"space": z + dz, "tm": t + dt}

    barrier = pltpu.get_barrier_semaphore()
    for step in range(1, space):
        pl.semaphore_signal(
            barrier, 1, device_id={"space": lax.rem(z + step, space), "tm": t}, device_id_type=MESH
        )
    for step in range(1, time):
        pl.semaphore_signal(
            barrier, 1, device_id={"space": z, "tm": lax.rem(t + step, time)}, device_id_type=MESH
        )
    for there, dz, dt in (
        (below & early, -1, -1), (below & late, -1, 1), (above & early, 1, -1), (above & late, 1, 1),
    ):
        @pl.when(there)
        def _(dz=dz, dt=dt):
            pl.semaphore_signal(barrier, 1, device_id=at(dz, dt), device_id_type=MESH)

    def side_by_side(values):
        return jnp.concatenate([values[n * width : (n + 1) * width] for n in range(frames)], axis=1)

    input_copy.wait()
    own = x_ref[...]
    xpack[...] = side_by_side(own)
    xbuf[1, cells:] = own

    def keep_x(piece, row, block):
        xts[piece, pl.ds(row, in_share)] = block

    transposed_slices(own.astype(jnp.float32), width, in_share, keep_x)
    xrecv[z, t] = xts[t]
    urecv[:, time * lanes :] = jnp.zeros((frames * out_share, lanes), jnp.bfloat16)
    nothing = jnp.zeros((frames * in_share, LANES), jnp.bfloat16)
    for pair_at in range(time):
        for col in range(3):
            xb[col, :, pair_at * lanes : pair_at * lanes + LANES] = nothing
            xb[6 + col, :, (pair_at + 1) * lanes - LANES : (pair_at + 1) * lanes] = nothing

    @pl.when(jnp.logical_not(early))
    def _():
        for row in range(3):
            xbuf[row, :cells] = jnp.zeros((cells, cin), jnp.bfloat16)

    @pl.when(jnp.logical_not(late))
    def _():
        for row in range(3):
            ubuf[row, cells:] = jnp.zeros((cells, cout), jnp.bfloat16)

    for missing, row in ((jnp.logical_not(below), 0), (jnp.logical_not(above), 2)):
        @pl.when(missing)
        def _(row=row):
            xbuf[row] = jnp.zeros((2 * cells, cin), jnp.bfloat16)
            ubuf[row] = jnp.zeros((2 * cells, cout), jnp.bfloat16)

    beside = (z + space - 1) // space + (2 * space - 2 - z) // space
    around = (t + time - 1) // time + (2 * time - 2 - t) // time
    pl.semaphore_wait(barrier, space + time - 2 + beside * around)

    def remote(source, target, send, recv, slot, device):
        return pltpu.make_async_remote_copy(
            src_ref=source, dst_ref=target, send_sem=send.at[slot], recv_sem=recv.at[slot],
            device_id=device, device_id_type=MESH,
        )

    def halos(pack, held, send, recv, ahead, there, here):
        cases = (
            (0, ahead, there, here),
            (1, 0, above, below),
            (-1, 0, below, above),
            (1, ahead, above & there, below & here),
            (-1, ahead, below & there, above & here),
        )
        return [
            (sent, got, 1 - dz, dt != 0,
             remote(pack, held.at[slot], send, recv, slot, at(dz, dt)))
            for slot, (dz, dt, sent, got) in enumerate(cases)
        ]

    def start_if(there, copy):
        @pl.when(there)
        def _():
            copy.start()

    def unpacked(halo, held, slot, buf, own_half):
        _, got, row, other_time, copy = halo
        half = 1 - own_half if other_time else own_half
        channels = buf.shape[2]

        @pl.when(got)
        def _():
            copy.wait_recv()
            for n in range(frames):
                place = half * cells + n * width
                buf[row, place : place + width] = held[slot, :, n * channels : (n + 1) * channels]

    x_halo = halos(xpack, xheld, hx_send, hx_recv, 1, late, early)
    for sent, _, _, _, copy in x_halo:
        start_if(sent, copy)

    x1, u1 = [], []
    for step in range(1, time):
        other = lax.rem(t + step, time)
        x1.append(remote(xts.at[other], xrecv.at[z, t], x1_send, x1_recv, step - 1,
                         {"space": z, "tm": other}))
    for step in range(1, space):
        other = lax.rem(z + step, space)
        window = urecv.at[:, pl.ds(pl.multiple_of(t * lanes + z * LANES, LANES), LANES)]
        u1.append(remote(uts.at[other], window, u1_send, u1_recv, step - 1,
                         {"space": other, "tm": t}))
    for copy in x1:
        copy.start()

    hops = []
    for step in range(space - 1):
        up, down = xrecv.at[z - step], xrecv.at[z + step]
        hops.append((
            (above & (z >= step), below & (z > step), z - 1 - step,
             remote(up, up, up_send, up_recv, step, at(1, 0))),
            (below & (z + step < space), above & (z + step + 1 < space), z + 1 + step,
             remote(down, down, down_send, down_recv, step, at(-1, 0))),
        ))

    couples = time // 2

    def gather(piece, source_time, slot, device_time):
        row = lax.rem(z + space - piece, space)
        start = pl.multiple_of(source_time * lanes + row * LANES, LANES)
        window = urecv.at[:, pl.ds(start, LANES)]
        return remote(window, window, u2_send, u2_recv, piece * (time - 1) + slot,
                      {"space": z, "tm": device_time})

    first, second = [], []
    for piece in range(space):
        first.append([gather(piece, t, 0, partner)])
        second.append([])
        for step in range(1, couples):
            came_from = lax.rem(t + time - 2 * step, time)
            first[piece].append(gather(piece, t, step, lax.rem(t + 2 * step, time)))
            second[piece].append(gather(piece, came_from, couples + step - 1, partner))

    def handed_on(piece):
        for held, copy in zip(first[piece][1:], second[piece]):
            held.wait_recv()
            copy.start()

    def taps(buf, row, depths, forward, totals):
        tap_row = row if forward else 2 - row
        for depth in depths:
            offset = (depth if forward else 2 - depth) * width
            window = buf[row, offset : offset + cells]
            for col in range(3):
                tap = w_ref[(depth * 3 + tap_row) * 3 + col]
                product = lax.dot_general(
                    window, tap, (((1,), (0 if forward else 1,)), ((), ())),
                    preferred_element_type=jnp.float32,
                )
                totals[col] = product if totals[col] is None else totals[col] + product

    def placed(row):
        for pair_at in range(time):
            held = xrecv[row, pair_at]
            wide = held.astype(jnp.float32)
            moved = (
                pltpu.roll(wide, 1, 1).astype(jnp.bfloat16),
                held,
                pltpu.roll(wide, LANES - 1, 1).astype(jnp.bfloat16),
            )
            for tap_row in range(3):
                place = row - tap_row + 1

                @pl.when((place >= 0) & (place < space))
                def _(tap_row=tap_row, place=place):
                    start = pl.multiple_of(pair_at * lanes + place * LANES, LANES)
                    for col in range(3):
                        xb[tap_row * 3 + col, :, pl.ds(start, LANES)] = moved[col]

    def hop_received(step):
        for _, got, _, copy in hops[step]:
            @pl.when(got)
            def _(copy=copy):
                copy.wait_recv()

    def hop_placed(step):
        for _, got, row, _ in hops[step]:
            @pl.when(got)
            def _(row=row):
                placed(row)

    weight_copy.wait()
    sums = [None, None, None]
    taps(xbuf, 1, (2,), True, sums)
    unpacked(x_halo[0], xheld, 0, xbuf, 1)
    taps(xbuf, 1, (0, 1), True, sums)
    for copy in x1:
        copy.wait_recv()
    for sent, _, _, copy in hops[0]:
        start_if(sent, copy)
    unpacked(x_halo[1], xheld, 1, xbuf, 1)
    taps(xbuf, 0, (2,), True, sums)
    unpacked(x_halo[2], xheld, 2, xbuf, 1)
    taps(xbuf, 2, (2,), True, sums)
    unpacked(x_halo[3], xheld, 3, xbuf, 1)
    taps(xbuf, 0, (0, 1), True, sums)
    unpacked(x_halo[4], xheld, 4, xbuf, 1)
    taps(xbuf, 2, (0, 1), True, sums)
    outputs = shifted_rows(sums[0], -1, width) + sums[1] + shifted_rows(sums[2], 1, width)
    logistic = jax.nn.sigmoid(outputs)
    derivative = logistic * (1.0 + outputs * (1.0 - logistic))
    cotangent_copy.wait()
    upstream = (g_ref[...].astype(jnp.float32) * derivative).astype(jnp.bfloat16)

    def keep_u(piece, row, block):
        uts[piece, pl.ds(row, out_share)] = block

    transposed_slices(upstream.astype(jnp.float32), width, out_share, keep_u)
    upack[...] = side_by_side(upstream)
    for copy in u1:
        copy.start()
    urecv[:, pl.ds(pl.multiple_of(t * lanes + z * LANES, LANES), LANES)] = uts[z]
    for copy in first[0]:
        copy.start()
    hop_received(0)
    if space > 2:
        for sent, _, _, copy in hops[1]:
            start_if(sent, copy)
    u_halo = halos(upack, uheld, hu_send, hu_recv, -1, early, late)
    for sent, _, _, _, copy in u_halo:
        start_if(sent, copy)
    ubuf[1, :cells] = upstream
    placed(z)
    sums = [None, None, None]
    taps(ubuf, 1, (2,), False, sums)

    for step in range(1, space):
        u1[step - 1].wait_recv()
        for copy in first[step]:
            copy.start()
    hop_placed(0)
    for step in range(1, space - 1):
        hop_received(step)
        if step + 1 < space - 1:
            for sent, _, _, copy in hops[step + 1]:
                start_if(sent, copy)
    handed_on(0)
    unpacked(u_halo[0], uheld, 0, ubuf, 0)
    taps(ubuf, 1, (0, 1), False, sums)
    for piece in range(1, space - 1):
        handed_on(piece)
    unpacked(u_halo[1], uheld, 1, ubuf, 0)
    taps(ubuf, 0, (2,), False, sums)
    handed_on(space - 1)
    unpacked(u_halo[2], uheld, 2, ubuf, 0)
    taps(ubuf, 2, (2,), False, sums)
    unpacked(u_halo[3], uheld, 3, ubuf, 0)
    taps(ubuf, 0, (0, 1), False, sums)
    unpacked(u_halo[4], uheld, 4, ubuf, 0)
    taps(ubuf, 2, (0, 1), False, sums)
    total = shifted_rows(sums[0], 1, width) + sums[1] + shifted_rows(sums[2], -1, width)
    ig_ref[...] = total.astype(jnp.bfloat16)
    for step in range(1, space - 1):
        hop_placed(step)

    for piece in range(space):
        first[piece][0].wait_recv()
        for copy in second[piece]:
            copy.wait_recv()
    both = jnp.concatenate([urecv[:, : time * lanes], urecv[:, lanes:]], axis=0)
    for tap_row in range(3):
        left = xb[tap_row * 3 : tap_row * 3 + 3].reshape(3 * frames * in_share, time * lanes)
        grads = lax.dot_general(
            left, both, (((1,), (1,)), ((), ())), preferred_element_type=jnp.float32
        ) * factor
        grads = grads.reshape(3, frames, in_share, 2 * frames * out_share)
        for col in range(3):
            joined = grads[col, 0, :, : 3 * out_share] + grads[col, 1, :, out_share:]
            for depth in range(3):
                lag = 2 - depth
                wg_ref[(depth * 3 + tap_row) * 3 + col] = joined[:, lag * out_share : (lag + 1) * out_share]

    for copy in x1 + u1 + sum(first, []) + sum(second, []):
        copy.wait_send()
    for sent, _, _, _, copy in x_halo + u_halo:
        @pl.when(sent)
        def _(copy=copy):
            copy.wait_send()
    for pair in hops:
        for sent, _, _, copy in pair:
            @pl.when(sent)
            def _(copy=copy):
                copy.wait_send()


def written(ig_ref, wg_ref, ig_out, wg_out, sems):
    copies = [
        pltpu.make_async_copy(wg_ref, wg_out, sems.at[0]),
        pltpu.make_async_copy(ig_ref, ig_out, sems.at[1]),
    ]
    for copy in copies:
        copy.start()
    for copy in copies:
        copy.wait()


def gathered(space, time, inputs, cotangent, weight):
    frames, _, width, cin = inputs.shape
    cout = cotangent.shape[3]
    cells = frames * width
    in_share, out_share = cin // time, cout // space
    lanes = space * LANES
    factor = 1.0 / math.sqrt(cells * space * time)
    vmem = pl.BlockSpec(memory_space=pltpu.VMEM)
    hbm = pl.BlockSpec(memory_space=pltpu.HBM)
    dma = pltpu.SemaphoreType.DMA
    bf16 = jnp.bfloat16
    input_grad, weight_grad = pl.pallas_call(
        functools.partial(kernel, space, time, width, factor),
        out_shape=(
            jax.ShapeDtypeStruct((cells, cin), bf16),
            jax.ShapeDtypeStruct((27, in_share, out_share), jnp.float32),
        ),
        in_specs=[hbm, hbm, hbm],
        out_specs=(vmem, vmem),
        scratch_shapes=[
            pltpu.VMEM((cells, cin), bf16),
            pltpu.VMEM((cells, cout), bf16),
            pltpu.VMEM((27, cin, cout), bf16),
            pltpu.VMEM((3, 2 * cells, cin), bf16),
            pltpu.VMEM((3, 2 * cells, cout), bf16),
            pltpu.VMEM((width, frames * cin), bf16),
            pltpu.VMEM((width, frames * cout), bf16),
            pltpu.VMEM((5, width, frames * cin), bf16),
            pltpu.VMEM((5, width, frames * cout), bf16),
            pltpu.VMEM((time, frames * in_share, LANES), bf16),
            pltpu.VMEM((space, frames * out_share, LANES), bf16),
            pltpu.VMEM((space, time, frames * in_share, LANES), bf16),
            pltpu.VMEM((frames * out_share, (time + 1) * lanes), bf16),
            pltpu.VMEM((9, frames * in_share, time * lanes), bf16),
            dma((3,)),
            dma((5,)), dma((5,)), dma((5,)), dma((5,)),
            dma((time - 1,)), dma((time - 1,)),
            dma((space - 1,)), dma((space - 1,)), dma((space - 1,)), dma((space - 1,)),
            dma((space - 1,)), dma((space - 1,)), dma((space * (time - 1),)), dma((space * (time - 1),)),
        ],
        compiler_params=pltpu.CompilerParams(
            collective_id=0, has_side_effects=True, vmem_limit_bytes=52 * 1024 * 1024
        ),
    )(inputs.reshape(cells, cin), cotangent.reshape(cells, cout), weight.reshape(27, cin, cout))
    input_grad, weight_grad = pl.pallas_call(
        written,
        out_shape=(
            jax.ShapeDtypeStruct(input_grad.shape, bf16),
            jax.ShapeDtypeStruct(weight_grad.shape, jnp.float32),
        ),
        in_specs=[vmem, vmem],
        out_specs=(hbm, hbm),
        scratch_shapes=[dma((2,))],
        compiler_params=pltpu.CompilerParams(vmem_limit_bytes=8 * 1024 * 1024),
    )(input_grad, weight_grad)
    return (
        input_grad.reshape(inputs.shape),
        weight_grad.reshape(3, 3, 3, in_share, out_share),
    )


def local(space, time, inputs, cotangent, weight):
    frames, rows, width, cin = inputs.shape
    cout = cotangent.shape[3]
    slices = 2 * frames * rows * width * space * time * (cin // time + cout // space)
    partials = 4 * 27 * cin * cout
    fits = (
        frames == 2
        and rows == 1
        and width < LANES
        and width % 16 == 0
        and space > 1
        and time % 2 == 0
        and (cin // time) % 16 == 0
        and (cout // space) % 16 == 0
    )
    if fits and slices < partials:
        return gathered(space, time, inputs, cotangent, weight)
    return reduced(inputs, cotangent, weight)


def solution(mesh):
    placed = (P(("rep", "tm"), "space", None, None), P(("rep", "tm"), "space", None, None), P())
    return jax.shard_map(
        functools.partial(local, mesh.shape["space"], mesh.shape["tm"]),
        mesh=mesh,
        in_specs=placed,
        out_specs=(
            P(("rep", "tm"), "space", None, None),
            P(None, None, None, ("rep", "tm"), "space"),
        ),
        check_vma=False,
    )
```

```python
import functools
import math

import jax
import jax.numpy as jnp
from jax import lax
from jax.experimental import pallas as pl
from jax.experimental.pallas import tpu as pltpu
from jax.sharding import PartitionSpec as P

MESH = pl.DeviceIdType.MESH
LANES = 128


def passed_along(array, axis, by):
    length = lax.axis_size(axis)
    pairs = [(i, i + by) for i in range(length) if 0 <= i + by < length]
    return lax.ppermute(array, axis, pairs)


def extended_2(cells, sides, width):
    for axis, dim in sides:
        count = lax.axis_size(axis)
        ends = count - 1
        head = lax.slice_in_dim(cells, 0, width, axis=dim)
        tail = lax.slice_in_dim(cells, cells.shape[dim] - width, cells.shape[dim], axis=dim)
        cells = jnp.concatenate(
            [
                lax.ppermute(tail, axis, [(i, (i + 1) % count) for i in range(ends)]),
                cells,
                lax.ppermute(head, axis, [((i + 1) % count, i) for i in range(ends)]),
            ],
            axis=dim,
        )
    return cells


def reduced(inputs, cotangent, weight):
    frame_count, row_count, col_count, in_channels = inputs.shape
    out_channels = cotangent.shape[3]
    cell_count = frame_count * row_count * col_count
    space_size = lax.axis_size("space")
    time_size = lax.axis_size("tm")
    factor = 1.0 / math.sqrt(cell_count * space_size * time_size)
    earlier = passed_along(inputs, "tm", 1)
    extended = jnp.concatenate([earlier, inputs], axis=0)
    rimmed = extended_2(extended, (("space", 1),), 1)
    padded = jnp.pad(rimmed, ((0, 0), (0, 0), (1, 1), (0, 0)))
    outputs = jnp.zeros((cell_count, out_channels), jnp.float32)
    for depth_tap in range(3):
        for row_tap in range(3):
            for col_tap in range(3):
                window = padded[
                    depth_tap : depth_tap + frame_count,
                    row_tap : row_tap + row_count,
                    col_tap : col_tap + col_count,
                ].reshape(cell_count, in_channels)
                outputs = outputs + jnp.dot(
                    window, weight[depth_tap, row_tap, col_tap], preferred_element_type=jnp.float32
                )
    logistic = jax.nn.sigmoid(outputs)
    derivative = logistic * (1.0 + outputs * (1.0 - logistic))
    upstream = (
        cotangent.reshape(cell_count, out_channels).astype(jnp.float32) * derivative
    ).astype(jnp.bfloat16)
    upstream_grid = upstream.reshape(frame_count, row_count, col_count, out_channels)
    arriving = passed_along(upstream_grid, "tm", -1)
    following = jnp.concatenate([upstream_grid, arriving], axis=0)
    following = extended_2(following, (("space", 1),), 1)
    following = jnp.pad(following, ((0, 0), (0, 0), (1, 1), (0, 0)))
    input_grad = jnp.zeros((cell_count, in_channels), jnp.float32)
    tap_grads = []
    for depth_tap in range(3):
        for row_tap in range(3):
            for col_tap in range(3):
                returned = following[
                    2 - depth_tap : 2 - depth_tap + frame_count,
                    2 - row_tap : 2 - row_tap + row_count,
                    2 - col_tap : 2 - col_tap + col_count,
                ].reshape(cell_count, out_channels)
                input_grad = input_grad + lax.dot_general(
                    returned,
                    weight[depth_tap, row_tap, col_tap],
                    (((1,), (1,)), ((), ())),
                    preferred_element_type=jnp.float32,
                )
                window = padded[
                    depth_tap : depth_tap + frame_count,
                    row_tap : row_tap + row_count,
                    col_tap : col_tap + col_count,
                ].reshape(cell_count, in_channels)
                tap_grads.append(
                    lax.dot_general(
                        window,
                        upstream,
                        (((0,), (0,)), ((), ())),
                        preferred_element_type=jnp.float32,
                    )
                )
    partial_grad = jnp.stack(tap_grads) * factor
    in_share = in_channels // time_size
    out_share = out_channels // space_size
    blocks = partial_grad.reshape(27, in_channels, space_size, out_share)
    blocks = blocks.transpose(2, 0, 1, 3).reshape(space_size * 27, in_channels, out_share)
    spatial_sum = lax.psum_scatter(blocks, "space", scatter_dimension=0, tiled=True)
    blocks = spatial_sum.reshape(27, time_size, in_share, out_share)
    blocks = blocks.transpose(1, 0, 2, 3).reshape(time_size * 27, in_share, out_share)
    owned_part = lax.psum_scatter(blocks, "tm", scatter_dimension=0, tiled=True)
    input_grad = input_grad.reshape(frame_count, row_count, col_count, in_channels).astype(
        jnp.bfloat16
    )
    return (input_grad, owned_part.reshape(3, 3, 3, in_share, out_share))


def shifted_rows(values, by, width):
    count = values.shape[0]
    rows = lax.broadcasted_iota(jnp.int32, values.shape, 0)
    edge = 0 if by < 0 else width - 1
    outside = rows == edge
    for frame in range(1, count // width):
        outside = outside | (rows == frame * width + edge)
    moved = pltpu.roll(values, 1 if by < 0 else count - 1, 0)
    return jnp.where(outside, 0.0, moved)


def transposed_slices(values, width, share, store):
    frames = values.shape[0] // width
    channels = values.shape[1]
    for frame in range(frames):
        part = values[frame * width : (frame + 1) * width]
        part = jnp.concatenate([part, jnp.zeros((LANES - width, channels), part.dtype)], axis=0)
        turned = part.T.astype(jnp.bfloat16)
        for piece in range(channels // share):
            store(piece, frame * share, turned[piece * share : (piece + 1) * share])


def kernel(
    space, time, width, factor,
    x_hbm, g_hbm, w_hbm, ig_ref, wg_ref,
    x_ref, g_ref, w_ref, xbuf, ubuf, xpack, upack, xheld, uheld, xts, uts, xrecv, urecv, xb,
    load_sem, hx_send, hx_recv, hu_send, hu_recv,
    x1_send, x1_recv, up_send, up_recv, down_send, down_recv, u1_send, u1_recv, u2_send, u2_recv,
):
    z = lax.axis_index("space")
    t = lax.axis_index("tm")
    cells, cin = x_ref.shape
    cout = g_ref.shape[1]
    in_share, out_share = cin // time, cout // space
    frames = cells // width
    lanes = space * LANES
    input_copy = pltpu.make_async_copy(x_hbm, x_ref, load_sem.at[0])
    weight_copy = pltpu.make_async_copy(w_hbm, w_ref, load_sem.at[1])
    cotangent_copy = pltpu.make_async_copy(g_hbm, g_ref, load_sem.at[2])
    for copy in (input_copy, weight_copy, cotangent_copy):
        copy.start()

    below, above = z > 0, z < space - 1
    early, late = t > 0, t < time - 1
    partner = t + 1 - 2 * lax.rem(t, 2)

    def at(dz, dt):
        return {"space": z + dz, "tm": t + dt}

    barrier = pltpu.get_barrier_semaphore()
    for step in range(1, space):
        pl.semaphore_signal(
            barrier, 1, device_id={"space": lax.rem(z + step, space), "tm": t}, device_id_type=MESH
        )
    for step in range(1, time):
        pl.semaphore_signal(
            barrier, 1, device_id={"space": z, "tm": lax.rem(t + step, time)}, device_id_type=MESH
        )
    for there, dz, dt in (
        (below & early, -1, -1), (below & late, -1, 1), (above & early, 1, -1), (above & late, 1, 1),
    ):
        @pl.when(there)
        def _(dz=dz, dt=dt):
            pl.semaphore_signal(barrier, 1, device_id=at(dz, dt), device_id_type=MESH)

    def side_by_side(values):
        return jnp.concatenate([values[n * width : (n + 1) * width] for n in range(frames)], axis=1)

    input_copy.wait()
    own = x_ref[...]
    xpack[...] = side_by_side(own)
    xbuf[1, cells:] = own

    def keep_x(piece, row, block):
        xts[piece, pl.ds(row, in_share)] = block

    transposed_slices(own.astype(jnp.float32), width, in_share, keep_x)
    xrecv[z, t] = xts[t]
    urecv[:, time * lanes :] = jnp.zeros((frames * out_share, lanes), jnp.bfloat16)
    nothing = jnp.zeros((frames * in_share, LANES), jnp.bfloat16)
    for pair_at in range(time):
        for col in range(3):
            xb[col, :, pair_at * lanes : pair_at * lanes + LANES] = nothing
            xb[6 + col, :, (pair_at + 1) * lanes - LANES : (pair_at + 1) * lanes] = nothing

    @pl.when(jnp.logical_not(early))
    def _():
        for row in range(3):
            xbuf[row, :cells] = jnp.zeros((cells, cin), jnp.bfloat16)

    @pl.when(jnp.logical_not(late))
    def _():
        for row in range(3):
            ubuf[row, cells:] = jnp.zeros((cells, cout), jnp.bfloat16)

    for missing, row in ((jnp.logical_not(below), 0), (jnp.logical_not(above), 2)):
        @pl.when(missing)
        def _(row=row):
            xbuf[row] = jnp.zeros((2 * cells, cin), jnp.bfloat16)
            ubuf[row] = jnp.zeros((2 * cells, cout), jnp.bfloat16)

    beside = (z + space - 1) // space + (2 * space - 2 - z) // space
    around = (t + time - 1) // time + (2 * time - 2 - t) // time
    pl.semaphore_wait(barrier, space + time - 2 + beside * around)

    def remote(source, target, send, recv, slot, device):
        return pltpu.make_async_remote_copy(
            src_ref=source, dst_ref=target, send_sem=send.at[slot], recv_sem=recv.at[slot],
            device_id=device, device_id_type=MESH,
        )

    def halos(pack, held, send, recv, ahead, there, here):
        cases = (
            (0, ahead, there, here),
            (1, 0, above, below),
            (-1, 0, below, above),
            (1, ahead, above & there, below & here),
            (-1, ahead, below & there, above & here),
        )
        return [
            (sent, got, 1 - dz, dt != 0,
             remote(pack, held.at[slot], send, recv, slot, at(dz, dt)))
            for slot, (dz, dt, sent, got) in enumerate(cases)
        ]

    def start_if(there, copy):
        @pl.when(there)
        def _():
            copy.start()

    def unpacked(halo, held, slot, buf, own_half):
        _, got, row, other_time, copy = halo
        half = 1 - own_half if other_time else own_half
        channels = buf.shape[2]

        @pl.when(got)
        def _():
            copy.wait_recv()
            for n in range(frames):
                place = half * cells + n * width
                buf[row, place : place + width] = held[slot, :, n * channels : (n + 1) * channels]

    x_halo = halos(xpack, xheld, hx_send, hx_recv, 1, late, early)
    for sent, _, _, _, copy in x_halo:
        start_if(sent, copy)

    x1, u1 = [], []
    for step in range(1, time):
        other = lax.rem(t + step, time)
        x1.append(remote(xts.at[other], xrecv.at[z, t], x1_send, x1_recv, step - 1,
                         {"space": z, "tm": other}))
    for step in range(1, space):
        other = lax.rem(z + step, space)
        window = urecv.at[:, pl.ds(pl.multiple_of(t * lanes + z * LANES, LANES), LANES)]
        u1.append(remote(uts.at[other], window, u1_send, u1_recv, step - 1,
                         {"space": other, "tm": t}))
    for copy in x1:
        copy.start()

    hops = []
    for step in range(space - 1):
        if step < 2:
            up, down, far, has_up, has_down = xrecv.at[z - step], xrecv.at[z + step], 1, z >= step, z + step < space
        else:
            up, down, far, has_up, has_down = xrecv.at[z], xrecv.at[z], step + 1, above, below
        hops.append((
            (has_up & (z + far < space), below & (z > step), z - 1 - step,
             remote(up, up, up_send, up_recv, step, at(far, 0))),
            (has_down & (z >= far), above & (z + step + 1 < space), z + 1 + step,
             remote(down, down, down_send, down_recv, step, at(-far, 0))),
        ))

    couples = time // 2

    def gather(piece, source_time, slot, device_time):
        row = lax.rem(z + space - piece, space)
        start = pl.multiple_of(source_time * lanes + row * LANES, LANES)
        window = urecv.at[:, pl.ds(start, LANES)]
        return remote(window, window, u2_send, u2_recv, piece * (time - 1) + slot,
                      {"space": z, "tm": device_time})

    first, second = [], []
    for piece in range(space):
        first.append([gather(piece, t, 0, partner)])
        second.append([])
        for step in range(1, couples):
            came_from = lax.rem(t + time - 2 * step, time)
            first[piece].append(gather(piece, t, step, lax.rem(t + 2 * step, time)))
            second[piece].append(gather(piece, came_from, couples + step - 1, partner))

    def handed_on(piece):
        for held, copy in zip(first[piece][1:], second[piece]):
            held.wait_recv()
            copy.start()

    def taps(buf, row, depths, forward, totals):
        tap_row = row if forward else 2 - row
        for depth in depths:
            offset = (depth if forward else 2 - depth) * width
            window = buf[row, offset : offset + cells]
            for col in range(3):
                tap = w_ref[(depth * 3 + tap_row) * 3 + col]
                product = lax.dot_general(
                    window, tap, (((1,), (0 if forward else 1,)), ((), ())),
                    preferred_element_type=jnp.float32,
                )
                totals[col] = product if totals[col] is None else totals[col] + product

    def placed(row):
        for pair_at in range(time):
            held = xrecv[row, pair_at]
            wide = held.astype(jnp.float32)
            moved = (
                pltpu.roll(wide, 1, 1).astype(jnp.bfloat16),
                held,
                pltpu.roll(wide, LANES - 1, 1).astype(jnp.bfloat16),
            )
            for tap_row in range(3):
                place = row - tap_row + 1

                @pl.when((place >= 0) & (place < space))
                def _(tap_row=tap_row, place=place):
                    start = pl.multiple_of(pair_at * lanes + place * LANES, LANES)
                    for col in range(3):
                        xb[tap_row * 3 + col, :, pl.ds(start, LANES)] = moved[col]

    def hop_received(step):
        for _, got, _, copy in hops[step]:
            @pl.when(got)
            def _(copy=copy):
                copy.wait_recv()

    def hop_placed(step):
        for _, got, row, _ in hops[step]:
            @pl.when(got)
            def _(row=row):
                placed(row)

    weight_copy.wait()
    sums = [None, None, None]
    taps(xbuf, 1, (2,), True, sums)
    unpacked(x_halo[0], xheld, 0, xbuf, 1)
    taps(xbuf, 1, (0, 1), True, sums)
    for copy in x1:
        copy.wait_recv()
    for sent, _, _, copy in hops[0]:
        start_if(sent, copy)
    unpacked(x_halo[1], xheld, 1, xbuf, 1)
    taps(xbuf, 0, (2,), True, sums)
    unpacked(x_halo[2], xheld, 2, xbuf, 1)
    taps(xbuf, 2, (2,), True, sums)
    unpacked(x_halo[3], xheld, 3, xbuf, 1)
    taps(xbuf, 0, (0, 1), True, sums)
    unpacked(x_halo[4], xheld, 4, xbuf, 1)
    taps(xbuf, 2, (0, 1), True, sums)
    outputs = shifted_rows(sums[0], -1, width) + sums[1] + shifted_rows(sums[2], 1, width)
    logistic = jax.nn.sigmoid(outputs)
    derivative = logistic * (1.0 + outputs * (1.0 - logistic))
    cotangent_copy.wait()
    upstream = (g_ref[...].astype(jnp.float32) * derivative).astype(jnp.bfloat16)

    def keep_u(piece, row, block):
        uts[piece, pl.ds(row, out_share)] = block

    transposed_slices(upstream.astype(jnp.float32), width, out_share, keep_u)
    upack[...] = side_by_side(upstream)
    for copy in u1:
        copy.start()
    urecv[:, pl.ds(pl.multiple_of(t * lanes + z * LANES, LANES), LANES)] = uts[z]
    for copy in first[0]:
        copy.start()
    hop_received(0)
    if space > 2:
        for sent, _, _, copy in hops[1]:
            start_if(sent, copy)
    u_halo = halos(upack, uheld, hu_send, hu_recv, -1, early, late)
    for sent, _, _, _, copy in u_halo:
        start_if(sent, copy)
    for hop in hops[2:]:
        for sent, _, _, copy in hop:
            start_if(sent, copy)
    ubuf[1, :cells] = upstream
    placed(z)
    sums = [None, None, None]
    taps(ubuf, 1, (2,), False, sums)

    for step in range(1, space):
        u1[step - 1].wait_recv()
        for copy in first[step]:
            copy.start()
    hop_placed(0)
    handed_on(0)
    unpacked(u_halo[0], uheld, 0, ubuf, 0)
    taps(ubuf, 1, (0, 1), False, sums)
    for piece in range(1, space - 1):
        handed_on(piece)
    unpacked(u_halo[1], uheld, 1, ubuf, 0)
    taps(ubuf, 0, (2,), False, sums)
    handed_on(space - 1)
    unpacked(u_halo[2], uheld, 2, ubuf, 0)
    taps(ubuf, 2, (2,), False, sums)
    unpacked(u_halo[3], uheld, 3, ubuf, 0)
    taps(ubuf, 0, (0, 1), False, sums)
    unpacked(u_halo[4], uheld, 4, ubuf, 0)
    taps(ubuf, 2, (0, 1), False, sums)
    total = shifted_rows(sums[0], 1, width) + sums[1] + shifted_rows(sums[2], -1, width)
    ig_ref[...] = total.astype(jnp.bfloat16)
    for step in range(1, space - 1):
        hop_received(step)
        hop_placed(step)

    for piece in range(space):
        first[piece][0].wait_recv()
        for copy in second[piece]:
            copy.wait_recv()
    both = jnp.concatenate([urecv[:, : time * lanes], urecv[:, lanes:]], axis=0)
    for tap_row in range(3):
        left = xb[tap_row * 3 : tap_row * 3 + 3].reshape(3 * frames * in_share, time * lanes)
        grads = lax.dot_general(
            left, both, (((1,), (1,)), ((), ())), preferred_element_type=jnp.float32
        ) * factor
        grads = grads.reshape(3, frames, in_share, 2 * frames * out_share)
        for col in range(3):
            joined = grads[col, 0, :, : 3 * out_share] + grads[col, 1, :, out_share:]
            for depth in range(3):
                lag = 2 - depth
                wg_ref[(depth * 3 + tap_row) * 3 + col] = joined[:, lag * out_share : (lag + 1) * out_share]

    for copy in x1 + u1 + sum(first, []) + sum(second, []):
        copy.wait_send()
    for sent, _, _, _, copy in x_halo + u_halo:
        @pl.when(sent)
        def _(copy=copy):
            copy.wait_send()
    for pair in hops:
        for sent, _, _, copy in pair:
            @pl.when(sent)
            def _(copy=copy):
                copy.wait_send()


def written(ig_ref, wg_ref, ig_out, wg_out, sems):
    copies = [
        pltpu.make_async_copy(wg_ref, wg_out, sems.at[0]),
        pltpu.make_async_copy(ig_ref, ig_out, sems.at[1]),
    ]
    for copy in copies:
        copy.start()
    for copy in copies:
        copy.wait()


def gathered(space, time, inputs, cotangent, weight):
    frames, _, width, cin = inputs.shape
    cout = cotangent.shape[3]
    cells = frames * width
    in_share, out_share = cin // time, cout // space
    lanes = space * LANES
    factor = 1.0 / math.sqrt(cells * space * time)
    vmem = pl.BlockSpec(memory_space=pltpu.VMEM)
    hbm = pl.BlockSpec(memory_space=pltpu.HBM)
    dma = pltpu.SemaphoreType.DMA
    bf16 = jnp.bfloat16
    input_grad, weight_grad = pl.pallas_call(
        functools.partial(kernel, space, time, width, factor),
        out_shape=(
            jax.ShapeDtypeStruct((cells, cin), bf16),
            jax.ShapeDtypeStruct((27, in_share, out_share), jnp.float32),
        ),
        in_specs=[hbm, hbm, hbm],
        out_specs=(vmem, vmem),
        scratch_shapes=[
            pltpu.VMEM((cells, cin), bf16),
            pltpu.VMEM((cells, cout), bf16),
            pltpu.VMEM((27, cin, cout), bf16),
            pltpu.VMEM((3, 2 * cells, cin), bf16),
            pltpu.VMEM((3, 2 * cells, cout), bf16),
            pltpu.VMEM((width, frames * cin), bf16),
            pltpu.VMEM((width, frames * cout), bf16),
            pltpu.VMEM((5, width, frames * cin), bf16),
            pltpu.VMEM((5, width, frames * cout), bf16),
            pltpu.VMEM((time, frames * in_share, LANES), bf16),
            pltpu.VMEM((space, frames * out_share, LANES), bf16),
            pltpu.VMEM((space, time, frames * in_share, LANES), bf16),
            pltpu.VMEM((frames * out_share, (time + 1) * lanes), bf16),
            pltpu.VMEM((9, frames * in_share, time * lanes), bf16),
            dma((3,)),
            dma((5,)), dma((5,)), dma((5,)), dma((5,)),
            dma((time - 1,)), dma((time - 1,)),
            dma((space - 1,)), dma((space - 1,)), dma((space - 1,)), dma((space - 1,)),
            dma((space - 1,)), dma((space - 1,)), dma((space * (time - 1),)), dma((space * (time - 1),)),
        ],
        compiler_params=pltpu.CompilerParams(
            collective_id=0, has_side_effects=True, vmem_limit_bytes=52 * 1024 * 1024
        ),
    )(inputs.reshape(cells, cin), cotangent.reshape(cells, cout), weight.reshape(27, cin, cout))
    input_grad, weight_grad = pl.pallas_call(
        written,
        out_shape=(
            jax.ShapeDtypeStruct(input_grad.shape, bf16),
            jax.ShapeDtypeStruct(weight_grad.shape, jnp.float32),
        ),
        in_specs=[vmem, vmem],
        out_specs=(hbm, hbm),
        scratch_shapes=[dma((2,))],
        compiler_params=pltpu.CompilerParams(vmem_limit_bytes=8 * 1024 * 1024),
    )(input_grad, weight_grad)
    return (
        input_grad.reshape(inputs.shape),
        weight_grad.reshape(3, 3, 3, in_share, out_share),
    )


def local(space, time, inputs, cotangent, weight):
    frames, rows, width, cin = inputs.shape
    cout = cotangent.shape[3]
    slices = 2 * frames * rows * width * space * time * (cin // time + cout // space)
    partials = 4 * 27 * cin * cout
    fits = (
        frames == 2
        and rows == 1
        and width < LANES
        and width % 16 == 0
        and space > 1
        and time % 2 == 0
        and (cin // time) % 16 == 0
        and (cout // space) % 16 == 0
    )
    if fits and slices < partials:
        return gathered(space, time, inputs, cotangent, weight)
    return reduced(inputs, cotangent, weight)


def solution(mesh):
    placed = (P(("rep", "tm"), "space", None, None), P(("rep", "tm"), "space", None, None), P())
    return jax.shard_map(
        functools.partial(local, mesh.shape["space"], mesh.shape["tm"]),
        mesh=mesh,
        in_specs=placed,
        out_specs=(
            P(("rep", "tm"), "space", None, None),
            P(None, None, None, ("rep", "tm"), "space"),
        ),
        check_vma=False,
    )
```
